128 devices in a mesh: op: 16 (over x, y), sec: 8 (over z, core).
Axes of the slice: x: 4, y: 4, z: 4, core: 2. Of those that a mesh axis runs over, the one named last changes fastest.
Arguments:
- wave: bfloat16 [32, 256, 4, 256], P('op'), may hold values from -6 to 6
- sector_dims: int32 [32], replicated, may hold values from 64 to 256, as said below
- left_ops: bfloat16 [32, 128, 256, 256], P(None, ('op', 'sec')), may hold values from -0.375 to 0.375
- right_ops: bfloat16 [32, 16, 8, 256, 256], P('op', None, 'sec'), may hold values from -0.375 to 0.375
- site_ops: float32 [128, 4, 4], replicated, may hold values from -0.25 to 0.25
Outputs:
- sigma: bfloat16 [32, 256, 4, 256], P('op', 'sec')
The draws below stay inside these ranges and needn't reach their ends.
Inputs may be any that keep to these rules, and one draw needn't show every extreme that they name: `sector_dims`: every entry is a multiple of 64, and at least one sector has exactly 256 states.
All inputs are finite; a program needn't handle non-finite values.
Results may differ from the reference program's by a relative error of at most 0.005.
Values may be sent and summed in bfloat16 or wider, within the bound.
No kernel may reach another device: no remote copies, remote signals or barrier semaphores. Data moves between devices by JAX's collectives and lax.ppermute only.
A program may use at most 128 MiB of HBM per device.

```python
import jax
import jax.numpy as jnp
from jax import lax

SECTORS = 32
BM = 256
GRAIN = 64
P_SIZE = 4
TERM_DEV = 1
TERMS = 128
N_OP = 16
N_SEC = 8


def draw_sector_dims(key, part):
    first_key, second_key = jax.random.split(key)
    counts = jax.random.randint(first_key, (SECTORS,), 1, BM // GRAIN + 1)
    chosen = jax.random.randint(second_key, (), 0, SECTORS)
    places = jnp.arange(SECTORS, dtype=jnp.int32)
    return jnp.where(places == chosen, BM, counts * GRAIN).astype(jnp.int32)


def level_of(key, dims, shards, low, top_value):
    level, own = 1.0, jax.random.fold_in(key, 6)
    for axis_at, blocks in shards:
        heights = jnp.exp(jax.random.uniform(jax.random.fold_in(own, axis_at), (blocks,), jnp.float32, low / len(shards), top_value / len(shards)))
        level = level * jnp.repeat(heights, dims[axis_at] // blocks).reshape([-1 if axis == axis_at else 1 for axis in range(len(dims))])
    return level


def normal_values(key, dims, width, limit, shards=(), kind=jnp.bfloat16):
    entries = width * jax.random.normal(key, dims, jnp.float32)
    if shards:
        entries = entries * level_of(key, dims, shards, -0.22, 0.18)
    return jnp.clip(entries, -limit, limit).astype(kind)


def setup_inputs(seed: int = 0) -> dict:
    streams_of = jax.random.split(jax.random.key(seed), 6)
    wave = normal_values(streams_of[0], (SECTORS, BM, P_SIZE, BM), 1.0, 6.0, ((0, 16),))
    sector_dims = draw_sector_dims(jax.random.fold_in(streams_of[5], 71), 0)
    left_ops = normal_values(streams_of[2], (SECTORS, TERMS, BM, BM), BM ** -0.5, 0.375, ((1, 128),))
    right_ops = normal_values(streams_of[3], (SECTORS, N_OP, N_SEC * TERM_DEV, BM, BM), BM ** -0.5, 0.375, ((0, 16), (2, 8)))
    site_ops = normal_values(streams_of[4], (TERMS, P_SIZE, P_SIZE), (P_SIZE * TERMS) ** -0.5, 0.25, (), jnp.float32)
    return {"wave": wave, "sector_dims": sector_dims, "left_ops": left_ops, "right_ops": right_ops, "site_ops": site_ops}


def reference(wave, sector_dims, left_ops, right_ops, site_ops):
    positions = jnp.arange(BM, dtype=jnp.int32)
    mask = (positions[None, :] < sector_dims[:, None]).astype(jnp.float32)
    masked = (wave.astype(jnp.float32) * mask[:, :, None, None] * mask[:, None, None, :]).astype(jnp.bfloat16)
    masked_wide = masked.astype(jnp.float32)
    right_all = right_ops.reshape(SECTORS, TERMS, BM, BM)

    def add_term(total, inputs):
        left_block, right_block, site_mat = inputs
        first = jnp.einsum('slm,smpr->slpr', left_block.astype(jnp.float32), masked_wide)
        second = jnp.einsum('slpr,qp->slqr', first, site_mat, precision=lax.Precision.HIGHEST)
        inter = second.astype(jnp.bfloat16)
        contrib = jnp.einsum('slqm,srm->slqr', inter.astype(jnp.float32), right_block.astype(jnp.float32))
        return total + contrib, None

    start = jnp.zeros((SECTORS, BM, P_SIZE, BM), jnp.float32)
    total, _ = lax.scan(add_term, start, (jnp.swapaxes(left_ops, 0, 1), jnp.swapaxes(right_all, 0, 1), site_ops))
    return (total * mask[:, :, None, None] * mask[:, None, None, :]).astype(jnp.bfloat16)
```

```python
import functools

import jax
import jax.numpy as jnp
from jax import lax
from jax.experimental import pallas as pl
from jax.experimental.pallas import tpu as pltpu
from jax.sharding import Mesh, PartitionSpec as P

CORES = 2
GROUP = 2


def sigma_kernel(z_count, group, meta, site_ref, left_ref, wave_ref, own_ref, other_ref, *refs):
    outs, total = refs[:z_count], refs[z_count]
    step = pl.program_id(0)
    core, z_at, sec_count = meta[0], meta[1], meta[2]

    @pl.when(step == 0)
    def _():
        total[...] = jnp.zeros_like(total)

    p_size = wave_ref.shape[0]
    mixed = [[] for _ in range(p_size)]
    rights = []
    for at in range(group):
        source = step * group + at
        for slot in range(CORES):
            side = core if slot == 0 else 1 - core
            term = source * sec_count + z_at * CORES + side
            left = left_ref[at * CORES + side]
            first = [
                jnp.dot(left, wave_ref[p], preferred_element_type=jnp.float32)
                for p in range(p_size)
            ]
            for q in range(p_size):
                second = first[0] * site_ref[term, q * p_size]
                for p in range(1, p_size):
                    second = second + first[p] * site_ref[term, q * p_size + p]
                mixed[q].append(second.astype(jnp.bfloat16))
            rights.append((own_ref if slot == 0 else other_ref)[0, at, 0])
    right = jnp.concatenate(rights, axis=1)
    for q in range(p_size):
        total[q] += lax.dot_general(
            jnp.concatenate(mixed[q], axis=1),
            right,
            (((1,), (1,)), ((), ())),
            preferred_element_type=jnp.float32,
        )

    @pl.when(step == pl.num_programs(0) - 1)
    def _():
        rows = total.shape[1] // z_count
        for shift in range(z_count):
            start = pl.multiple_of(lax.rem(z_at + shift, z_count) * rows, rows)
            block = total[:, pl.ds(start, rows), :]
            outs[shift][...] = block.astype(outs[shift].dtype)


def sigma_call(meta, site, left, wave, own, other, z_count):
    sources, width = own.shape[1], own.shape[-1]
    p_size = wave.shape[0]
    rows = width // z_count
    group = GROUP
    right_spec = pl.BlockSpec(
        (1, group, 1, width, width), lambda step, meta: (meta[0], step, 0, 0, 0)
    )
    return pl.pallas_call(
        functools.partial(sigma_kernel, z_count, group),
        grid_spec=pltpu.PrefetchScalarGridSpec(
            num_scalar_prefetch=1,
            grid=(sources // group,),
            in_specs=[
                pl.BlockSpec(memory_space=pltpu.SMEM),
                pl.BlockSpec((group * CORES, width, width), lambda step, meta: (step, 0, 0)),
                pl.BlockSpec((p_size, width, width), lambda step, meta: (0, 0, 0)),
                right_spec,
                right_spec,
            ],
            out_specs=[
                pl.BlockSpec((p_size, rows, width), lambda step, meta: (0, 0, 0))
            ] * z_count,
            scratch_shapes=[pltpu.VMEM((p_size, width, width), jnp.float32)],
        ),
        out_shape=[
            jax.ShapeDtypeStruct((p_size, rows, width), jnp.float32 if s == 0 else jnp.bfloat16)
            for s in range(z_count)
        ],
        compiler_params=pltpu.CompilerParams(
            dimension_semantics=("arbitrary",), vmem_limit_bytes=48 << 20
        ),
        name="sigma_terms",
    )(meta, site, left, wave, own, other)


def shards(wave, sector_dims, left_ops, right_ops, site_ops):
    z_count = lax.axis_size("z")
    op_at, z_at, core = lax.axis_index("op"), lax.axis_index("z"), lax.axis_index("core")
    width, p_size = wave.shape[1], wave.shape[2]
    swap = [(0, 1), (1, 0)]

    other = lax.ppermute(right_ops, "core", swap)
    left = lax.all_to_all(left_ops[:, 0], ("op", "core"), split_axis=0, concat_axis=0, tiled=True)

    size = lax.dynamic_slice_in_dim(sector_dims, op_at * CORES + core, 1)
    mask = (lax.iota(jnp.int32, width) < size).astype(jnp.float32)
    block = lax.dynamic_index_in_dim(wave, core, 0, keepdims=False)
    masked = block.astype(jnp.float32) * mask[:, None, None] * mask[None, None, :]
    masked = masked.astype(jnp.bfloat16).transpose(1, 0, 2)

    meta = jnp.stack([core, z_at, jnp.int32(z_count * CORES)]).astype(jnp.int32)
    site = site_ops.reshape(site_ops.shape[0], -1)
    parts = sigma_call(meta, site, left, masked, right_ops, other, z_count)

    total = parts[0]
    for shift in range(1, z_count):
        ring = [(z, (z + shift) % z_count) for z in range(z_count)]
        total = total + lax.ppermute(parts[shift], "z", ring).astype(jnp.float32)

    rows = width // z_count
    row_mask = lax.dynamic_slice_in_dim(mask, z_at * rows, rows)
    share = (total * row_mask[None, :, None] * mask[None, None, :]).astype(jnp.bfloat16)
    share = share.transpose(1, 0, 2).reshape(CORES, rows // CORES, p_size, width)
    keep = lax.dynamic_index_in_dim(share, core, 0, keepdims=False)
    give = lax.dynamic_index_in_dim(share, 1 - core, 0, keepdims=False)
    take = lax.ppermute(give, "core", swap)
    first = core == 0
    return jnp.stack([jnp.where(first, keep, take), jnp.where(first, take, keep)])


def solution(mesh):
    op_count, sec_count = mesh.shape["op"], mesh.shape["sec"]
    split = Mesh(
        mesh.devices.reshape(op_count, sec_count // CORES, CORES), ("op", "z", "core")
    )
    placed = (
        P("op", None, None, None),
        P(),
        P(None, ("op", "z", "core"), None, None),
        P("op", None, ("z", "core"), None, None),
        P(),
    )
    return jax.shard_map(
        shards, mesh=split, in_specs=placed,
        out_specs=P("op", ("z", "core"), None, None), check_vma=False,
    )
```

```python
import functools

import jax
import jax.numpy as jnp
from jax import lax
from jax.experimental import pallas as pl
from jax.experimental.pallas import tpu as pltpu
from jax.sharding import Mesh, PartitionSpec as P

CORES = 2
GROUP = 2
ROWS = 16
LEFT_TERMS = 2
VMEM_LIMIT = 48 << 20


def right_kernel(group, meta, site_ref, wave_ref, own_ref, other_ref, held_ref, first):
    step = pl.program_id(0)
    core, z_at, sec_count = meta[0], meta[1], meta[2]
    p_size, width = wave_ref.shape[0], wave_ref.shape[1]
    waves = wave_ref[...].reshape(p_size * width, width)
    for at in range(group):
        source = step * group + at
        for slot in range(CORES):
            side = core if slot == 0 else 1 - core
            term = source * sec_count + z_at * CORES + side
            buf = (at * CORES + slot) % 2
            first[buf] = lax.dot_general(
                waves, (own_ref if slot == 0 else other_ref)[0, at, 0],
                (((1,), (1,)), ((), ())), preferred_element_type=jnp.float32,
            )
            scale = [[site_ref[term, q * p_size + p] for p in range(p_size)] for q in range(p_size)]
            place = at * CORES + side
            for low in range(0, width, ROWS):
                parts = [first[buf, p * width + low : p * width + low + ROWS] for p in range(p_size)]
                for q in range(p_size):
                    second = parts[0] * scale[q][0]
                    for p in range(1, p_size):
                        second = second + parts[p] * scale[q][p]
                    held_ref[place, low : low + ROWS, q * width : (q + 1) * width] = second.astype(
                        jnp.bfloat16
                    )


def right_call(meta, site, wave, own, other):
    sources, width = own.shape[1], own.shape[-1]
    p_size = wave.shape[0]
    right_spec = pl.BlockSpec(
        (1, GROUP, 1, width, width), lambda step, meta: (meta[0], step, 0, 0, 0)
    )
    return pl.pallas_call(
        functools.partial(right_kernel, GROUP),
        grid_spec=pltpu.PrefetchScalarGridSpec(
            num_scalar_prefetch=1,
            grid=(sources // GROUP,),
            in_specs=[
                pl.BlockSpec(memory_space=pltpu.SMEM),
                pl.BlockSpec((p_size, width, width), lambda step, meta: (0, 0, 0)),
                right_spec,
                right_spec,
            ],
            out_specs=pl.BlockSpec(
                (GROUP * CORES, width, p_size * width), lambda step, meta: (step, 0, 0)
            ),
            scratch_shapes=[pltpu.VMEM((2, p_size * width, width), jnp.float32)],
        ),
        out_shape=jax.ShapeDtypeStruct((sources * CORES, width, p_size * width), jnp.bfloat16),
        compiler_params=pltpu.CompilerParams(vmem_limit_bytes=VMEM_LIMIT),
        name="right_terms",
    )(meta, site, wave, own, other)


def left_kernel(z_count, p_size, meta, left_hbm, held_hbm, *refs):
    outs = refs[:z_count]
    left, held, total, left_sem, held_sem = refs[z_count:]
    z_at = meta[1]
    terms, width = left.shape[0], left.shape[1]
    copies = []
    for at in range(0, terms, LEFT_TERMS):
        span = pl.ds(at, LEFT_TERMS)
        slot = at // LEFT_TERMS
        pair = (
            pltpu.make_async_copy(left_hbm.at[span], left.at[span], left_sem.at[slot]),
            pltpu.make_async_copy(held_hbm.at[span], held.at[span], held_sem.at[slot]),
        )
        for copy in pair:
            copy.start()
        copies.append(pair)

    for slot, pair in enumerate(copies):
        for copy in pair:
            copy.wait()
        add = None
        for at in range(slot * LEFT_TERMS, (slot + 1) * LEFT_TERMS):
            product = jnp.dot(left[at], held[at], preferred_element_type=jnp.float32)
            add = product if add is None else add + product
        if slot == 0:
            total[...] = add
        else:
            total[...] += add

    rows = width // z_count
    for shift in range(z_count):
        start = pl.multiple_of(lax.rem(z_at + shift, z_count) * rows, rows)
        block = total[pl.ds(start, rows), :]
        for q in range(p_size):
            outs[shift][q] = block[:, q * width : (q + 1) * width].astype(outs[shift].dtype)


def left_call(meta, left, held, z_count):
    terms, width, columns = held.shape
    p_size = columns // width
    rows = width // z_count
    return pl.pallas_call(
        functools.partial(left_kernel, z_count, p_size),
        in_specs=[
            pl.BlockSpec(memory_space=pltpu.SMEM),
            pl.BlockSpec(memory_space=pl.ANY),
            pl.BlockSpec(memory_space=pl.ANY),
        ],
        out_specs=[pl.BlockSpec(memory_space=pltpu.VMEM)] * z_count,
        out_shape=[
            jax.ShapeDtypeStruct((p_size, rows, width), jnp.float32 if s == 0 else jnp.bfloat16)
            for s in range(z_count)
        ],
        scratch_shapes=[
            pltpu.VMEM((terms, width, width), jnp.bfloat16),
            pltpu.VMEM((terms, width, columns), jnp.bfloat16),
            pltpu.VMEM((width, columns), jnp.float32),
            pltpu.SemaphoreType.DMA((terms // LEFT_TERMS,)),
            pltpu.SemaphoreType.DMA((terms // LEFT_TERMS,)),
        ],
        compiler_params=pltpu.CompilerParams(vmem_limit_bytes=VMEM_LIMIT),
        name="left_terms",
    )(meta, left, held)


def shards(wave, sector_dims, left_ops, right_ops, site_ops):
    z_count = lax.axis_size("z")
    op_at, z_at, core = lax.axis_index("op"), lax.axis_index("z"), lax.axis_index("core")
    width, p_size = wave.shape[1], wave.shape[2]
    swap = [(0, 1), (1, 0)]

    other = lax.ppermute(right_ops, "core", swap)
    left = lax.all_to_all(left_ops[:, 0], ("op", "core"), split_axis=0, concat_axis=0, tiled=True)

    size = lax.dynamic_slice_in_dim(sector_dims, op_at * CORES + core, 1)
    mask = (lax.iota(jnp.int32, width) < size).astype(jnp.float32)
    block = lax.dynamic_index_in_dim(wave, core, 0, keepdims=False)
    masked = block.astype(jnp.float32) * mask[:, None, None] * mask[None, None, :]
    masked = masked.astype(jnp.bfloat16).transpose(1, 0, 2)

    meta = jnp.stack([core, z_at, jnp.int32(z_count * CORES)]).astype(jnp.int32)
    site = site_ops.reshape(site_ops.shape[0], -1)
    held = right_call(meta, site, masked, right_ops, other)
    parts = left_call(meta, left, held, z_count)

    total = parts[0]
    for shift in sorted(range(1, z_count), key=lambda s: -min(s, z_count - s)):
        ring = [(z, (z + shift) % z_count) for z in range(z_count)]
        total = total + lax.ppermute(parts[shift], "z", ring).astype(jnp.float32)

    rows = width // z_count
    row_mask = lax.dynamic_slice_in_dim(mask, z_at * rows, rows)
    share = (total * row_mask[None, :, None] * mask[None, None, :]).astype(jnp.bfloat16)
    share = share.transpose(1, 0, 2).reshape(CORES, rows // CORES, p_size, width)
    keep = lax.dynamic_index_in_dim(share, core, 0, keepdims=False)
    give = lax.dynamic_index_in_dim(share, 1 - core, 0, keepdims=False)
    take = lax.ppermute(give, "core", swap)
    first = core == 0
    return jnp.stack([jnp.where(first, keep, take), jnp.where(first, take, keep)])


def solution(mesh):
    op_count, sec_count = mesh.shape["op"], mesh.shape["sec"]
    split = Mesh(
        mesh.devices.reshape(op_count, sec_count // CORES, CORES), ("op", "z", "core")
    )
    placed = (
        P("op", None, None, None),
        P(),
        P(None, ("op", "z", "core"), None, None),
        P("op", None, ("z", "core"), None, None),
        P(),
    )
    return jax.shard_map(
        shards, mesh=split, in_specs=placed,
        out_specs=P("op", ("z", "core"), None, None), check_vma=False,
    )
```

```python
import functools
import math

import jax
import jax.numpy as jnp
from jax import lax
from jax.experimental import pallas as pl
from jax.experimental.pallas import tpu as pltpu
from jax.sharding import Mesh, PartitionSpec as P

CORES = 2
ROWS = 16
STEP_TERMS = 2
VMEM_LIMIT = 16 << 20
IN_VMEM = pl.BlockSpec(memory_space=pltpu.VMEM)
IN_SMEM = pl.BlockSpec(memory_space=pltpu.SMEM)


def right_kernel(count, first_term, meta, site_ref, wave_ref, *refs):
    rights, held_ref, first = refs[:count], refs[count], refs[count + 1]
    step = pl.program_id(0)
    p_size, width = wave_ref.shape[1], wave_ref.shape[2]
    waves = wave_ref[0].reshape(p_size * width, width)
    for at in range(count):
        term = meta[1] + meta[2] * meta[3 + first_term + step * count + at]
        first[at] = lax.dot_general(
            waves, rights[at][0, 0, 0], (((1,), (1,)), ((), ())),
            preferred_element_type=jnp.float32,
        )
        scale = [[site_ref[term, q * p_size + p] for p in range(p_size)] for q in range(p_size)]
        for low in range(0, width, ROWS):
            parts = [first[at, p * width + low : p * width + low + ROWS] for p in range(p_size)]
            for q in range(p_size):
                second = parts[0] * scale[q][0]
                for p in range(1, p_size):
                    second = second + parts[p] * scale[q][p]
                held_ref[at, low : low + ROWS, q * width : (q + 1) * width] = second.astype(
                    jnp.bfloat16
                )


def right_call(meta, site, wave, right, sector, first_term, terms):
    width, p_size = right.shape[-1], wave.shape[1]
    count = STEP_TERMS

    def right_at(at, step, meta):
        return sector, meta[3 + first_term + step * count + at], 0, 0, 0

    return pl.pallas_call(
        functools.partial(right_kernel, count, first_term),
        grid_spec=pltpu.PrefetchScalarGridSpec(
            num_scalar_prefetch=1,
            grid=(terms // count,),
            in_specs=[
                IN_SMEM,
                pl.BlockSpec((1, p_size, width, width), lambda step, meta: (sector, 0, 0, 0)),
            ]
            + [
                pl.BlockSpec((1, 1, 1, width, width), functools.partial(right_at, at))
                for at in range(count)
            ],
            out_specs=pl.BlockSpec(
                (count, width, p_size * width), lambda step, meta: (step, 0, 0)
            ),
            scratch_shapes=[pltpu.VMEM((count, p_size * width, width), jnp.float32)],
        ),
        out_shape=jax.ShapeDtypeStruct((terms, width, p_size * width), jnp.bfloat16),
        compiler_params=pltpu.CompilerParams(vmem_limit_bytes=VMEM_LIMIT),
        name="right_terms",
    )(meta, site, wave, *[right] * count)


def left_sum(blocks, helds, places):
    add = None
    for block, block_at, held, held_at in places:
        product = jnp.dot(
            blocks[block][block_at], helds[held][held_at], preferred_element_type=jnp.float32
        )
        add = product if add is None else add + product
    return add


def start_kernel(n_blocks, n_helds, places, *refs):
    blocks, helds = refs[:n_blocks], refs[n_blocks : n_blocks + n_helds]
    refs[-1][...] = left_sum(blocks, helds, places)


def finish_kernel(n_blocks, n_helds, places, z_count, p_size, meta, total_ref, *refs):
    blocks, helds = refs[:n_blocks], refs[n_blocks : n_blocks + n_helds]
    keep_ref, give_ref, total = refs[n_blocks + n_helds :]
    total[...] = total_ref[...] + left_sum(blocks, helds, places)
    width = total.shape[0]
    rows = width // (z_count * CORES)
    for shift in range(z_count):
        z_to = lax.rem(meta[0] + shift, z_count)
        for out, core in ((keep_ref, meta[1] % CORES), (give_ref, 1 - meta[1] % CORES)):
            start = pl.multiple_of((z_to * CORES + core) * rows, rows)
            block = total[pl.ds(start, rows), :]
            for q in range(p_size):
                out[shift, q] = block[:, q * width : (q + 1) * width].astype(out.dtype)


def join_kernel(keep_ref, take_ref, *outs):
    for shift, out in enumerate(outs):
        out[...] = (keep_ref[shift] + take_ref[shift].astype(jnp.float32)).astype(out.dtype)


def left_start(blocks, helds, places):
    width, columns = helds[0].shape[1:]
    return pl.pallas_call(
        functools.partial(start_kernel, len(blocks), len(helds), places),
        in_specs=[IN_VMEM] * (len(blocks) + len(helds)),
        out_specs=IN_VMEM,
        out_shape=jax.ShapeDtypeStruct((width, columns), jnp.float32),
        compiler_params=pltpu.CompilerParams(vmem_limit_bytes=VMEM_LIMIT),
        name="left_start",
    )(*blocks, *helds)


def left_finish(meta, total, blocks, helds, places, z_count):
    width, columns = helds[0].shape[1:]
    p_size = columns // width
    shape = (z_count, p_size, width // (z_count * CORES), width)
    return pl.pallas_call(
        functools.partial(finish_kernel, len(blocks), len(helds), places, z_count, p_size),
        in_specs=[IN_SMEM, IN_VMEM] + [IN_VMEM] * (len(blocks) + len(helds)),
        out_specs=[IN_VMEM, IN_VMEM],
        out_shape=[
            jax.ShapeDtypeStruct(shape, jnp.float32),
            jax.ShapeDtypeStruct(shape, jnp.bfloat16),
        ],
        scratch_shapes=[pltpu.VMEM((width, columns), jnp.float32)],
        compiler_params=pltpu.CompilerParams(vmem_limit_bytes=VMEM_LIMIT),
        name="left_finish",
    )(meta, total, *blocks, *helds)


def join_call(keep, take):
    z_count, shape = keep.shape[0], keep.shape[1:]
    return pl.pallas_call(
        join_kernel,
        in_specs=[IN_VMEM, IN_VMEM],
        out_specs=[IN_VMEM] * z_count,
        out_shape=[
            jax.ShapeDtypeStruct(shape, jnp.float32 if s == 0 else jnp.bfloat16)
            for s in range(z_count)
        ],
        compiler_params=pltpu.CompilerParams(vmem_limit_bytes=VMEM_LIMIT),
        name="join_cores",
    )(keep, take)


def shards(wave, sector_dims, left_ops, right_ops, site_ops):
    op_count, z_count = lax.axis_size("op"), lax.axis_size("z")
    side = math.isqrt(op_count)
    op_at, z_at, core = lax.axis_index("op"), lax.axis_index("z"), lax.axis_index("core")
    sectors, width, p_size = wave.shape[0], wave.shape[1], wave.shape[2]
    swap = [(0, 1), (1, 0)]

    x_at, y_at = op_at // side, op_at % side
    near_at, far_at = jnp.where(core == 0, x_at, y_at), jnp.where(core == 0, y_at, x_at)

    def place(near, far):
        near, far = near % side, far % side
        return jnp.where(core == 0, near * side + far, far * side + near)

    def ring(shift, first):
        pairs = []
        for op in range(op_count):
            for c in range(CORES):
                x, y = op // side, op % side
                if (c == 0) == first:
                    x = (x + shift) % side
                else:
                    y = (y + shift) % side
                pairs.append((op * CORES + c, (x * side + y) * CORES + c))
        return pairs

    order = [0] + sorted(range(1, side), key=lambda s: min(s, side - s))
    last = order[-1]
    left = left_ops.reshape(left_ops.shape[0], width, width)
    sent = [[None] * side for _ in range(sectors)]
    for sector in range(sectors):
        for shift in order:
            sent[sector][shift] = jnp.concatenate(
                [
                    lax.dynamic_slice_in_dim(
                        left, place(near_at + shift, far_at + turn) * sectors + sector, 1
                    )
                    for turn in range(side)
                ]
            )
    arrived = [[None] * side for _ in range(sectors)]
    forwarded = [[None] * side for _ in range(sectors)]
    for sector in range(sectors):
        arrived[sector][0] = sent[sector][0]
        for shift in order[1:]:
            arrived[sector][shift] = lax.ppermute(
                sent[sector][shift], ("op", "core"), ring(shift, True)
            )
        for turn in order[1:]:
            forwarded[sector][turn] = lax.ppermute(
                jnp.stack([arrived[sector][shift][turn] for shift in range(side)]),
                ("op", "core"),
                ring(turn, False),
            )

    sizes = lax.dynamic_slice_in_dim(sector_dims, op_at * sectors, sectors)
    mask = (lax.broadcasted_iota(jnp.int32, (sectors, width), 1) < sizes[:, None]).astype(
        jnp.float32
    )
    masked = wave.astype(jnp.float32) * mask[:, :, None, None] * mask[:, None, None, :]
    masked = masked.astype(jnp.bfloat16).transpose(0, 2, 1, 3)
    site = site_ops.reshape(site_ops.shape[0], -1)
    sources = [place(near_at - shift, far_at - turn) for turn in range(side) for shift in range(side)]
    meta = jnp.stack(
        [z_at, z_at * CORES + core, jnp.int32(z_count * CORES)] + sources
    ).astype(jnp.int32)

    rows = width // (z_count * CORES)
    own_rows = (z_at * CORES + core) * rows
    shares = []
    for sector in range(sectors):
        half = side // 2 * side
        helds = [
            right_call(meta, site, masked, right_ops, sector, part * half, half)
            for part in range(2)
        ]

        def held_place(turn, shift):
            at = turn * side + shift
            return at // half, at % half

        early = [(shift, 0, *held_place(0, shift)) for shift in range(side)]
        blocks = list(arrived[sector])
        for turn in order[1:-1]:
            early += [(len(blocks), shift, *held_place(turn, shift)) for shift in range(side)]
            blocks.append(forwarded[sector][turn])
        total = left_start(blocks, helds, early)
        held_at = held_place(last, 0)
        late = [(0, shift, 0, held_at[1] + shift) for shift in range(side)]
        keep, give = left_finish(
            meta, total, [forwarded[sector][last]], [helds[held_at[0]]], late, z_count
        )
        parts = join_call(keep, lax.ppermute(give, "core", swap))
        summed = parts[0]
        for shift in sorted(range(1, z_count), key=lambda s: -min(s, z_count - s)):
            z_ring = [(z, (z + shift) % z_count) for z in range(z_count)]
            summed = summed + lax.ppermute(parts[shift], "z", z_ring).astype(jnp.float32)
        row_mask = lax.dynamic_slice_in_dim(mask[sector], own_rows, rows)
        share = summed * row_mask[None, :, None] * mask[sector][None, None, :]
        shares.append(share.astype(jnp.bfloat16).transpose(1, 0, 2))
    return jnp.stack(shares)


def solution(mesh):
    op_count, sec_count = mesh.shape["op"], mesh.shape["sec"]
    split = Mesh(
        mesh.devices.reshape(op_count, sec_count // CORES, CORES), ("op", "z", "core")
    )
    placed = (
        P("op", None, None, None),
        P(),
        P(None, ("op", "z", "core"), None, None),
        P("op", None, ("z", "core"), None, None),
        P(),
    )
    return jax.shard_map(
        shards, mesh=split, in_specs=placed,
        out_specs=P("op", ("z", "core"), None, None), check_vma=False,
    )
```

```python
import functools

import jax
import jax.numpy as jnp
from jax import lax
from jax.experimental import pallas as pl
from jax.experimental.pallas import tpu as pltpu
from jax.sharding import Mesh, PartitionSpec as P

CORES = 2
GROUP = 2
ROWS = 16
LEFT_TERMS = 2
VMEM_LIMIT = 48 << 20


def right_kernel(group, meta, site_ref, wave_ref, right_ref, held_ref, first):
    source = pl.program_id(1) * group
    p_size, width = wave_ref.shape[1], wave_ref.shape[2]
    waves = wave_ref[0].reshape(p_size * width, width)
    for at in range(group):
        term = (source + at) * meta[2] + meta[1]
        buf = at % 2
        first[buf] = lax.dot_general(
            waves, right_ref[0, at, 0], (((1,), (1,)), ((), ())),
            preferred_element_type=jnp.float32,
        )
        scale = [[site_ref[term, q * p_size + p] for p in range(p_size)] for q in range(p_size)]
        for low in range(0, width, ROWS):
            parts = [first[buf, p * width + low : p * width + low + ROWS] for p in range(p_size)]
            for q in range(p_size):
                second = parts[0] * scale[q][0]
                for p in range(1, p_size):
                    second = second + parts[p] * scale[q][p]
                held_ref[0, at, low : low + ROWS, q * width : (q + 1) * width] = second.astype(
                    jnp.bfloat16
                )


def right_call(meta, site, wave, right):
    sectors, sources, width = right.shape[0], right.shape[1], right.shape[-1]
    p_size = wave.shape[1]
    return pl.pallas_call(
        functools.partial(right_kernel, GROUP),
        grid=(sectors, sources // GROUP),
        in_specs=[
            pl.BlockSpec(memory_space=pltpu.SMEM),
            pl.BlockSpec(memory_space=pltpu.SMEM),
            pl.BlockSpec((1, p_size, width, width), lambda sector, step: (sector, 0, 0, 0)),
            pl.BlockSpec((1, GROUP, 1, width, width), lambda sector, step: (sector, step, 0, 0, 0)),
        ],
        out_specs=pl.BlockSpec(
            (1, GROUP, width, p_size * width), lambda sector, step: (sector, step, 0, 0)
        ),
        out_shape=jax.ShapeDtypeStruct((sectors, sources, width, p_size * width), jnp.bfloat16),
        scratch_shapes=[pltpu.VMEM((2, p_size * width, width), jnp.float32)],
        compiler_params=pltpu.CompilerParams(vmem_limit_bytes=VMEM_LIMIT),
        name="right_terms",
    )(meta, site, wave, right)


def left_kernel(z_count, p_size, meta, left_hbm, held_hbm, keep_ref, give_ref, *scratch):
    left, held, total, left_sem, held_sem = scratch
    sectors, sources = held.shape[0], held.shape[1]
    width = total.shape[0]
    rows = width // (z_count * CORES)
    core = lax.rem(meta[1], CORES)
    steps = sources // LEFT_TERMS
    copies = []
    for sector in range(sectors):
        for step in range(steps):
            span = pl.ds(step * LEFT_TERMS, LEFT_TERMS)
            slot = sector * steps + step
            pair = (
                pltpu.make_async_copy(
                    left_hbm.at[span, sector], left.at[sector, span], left_sem.at[slot]
                ),
                pltpu.make_async_copy(
                    held_hbm.at[sector, span], held.at[sector, span], held_sem.at[slot]
                ),
            )
            for copy in pair:
                copy.start()
            copies.append(pair)

    for sector in range(sectors):
        for step in range(steps):
            for copy in copies[sector * steps + step]:
                copy.wait()
            add = None
            for at in range(step * LEFT_TERMS, (step + 1) * LEFT_TERMS):
                product = jnp.dot(
                    left[sector, at], held[sector, at], preferred_element_type=jnp.float32
                )
                add = product if add is None else add + product
            if step == 0:
                total[...] = add
            else:
                total[...] += add
        for shift in range(z_count):
            z_to = lax.rem(meta[0] + shift, z_count)
            for out, side in ((keep_ref, core), (give_ref, 1 - core)):
                start = pl.multiple_of((z_to * CORES + side) * rows, rows)
                block = total[pl.ds(start, rows), :]
                for q in range(p_size):
                    out[shift, sector, q] = block[:, q * width : (q + 1) * width].astype(out.dtype)


def left_call(meta, left, held, z_count):
    sectors, sources, width, columns = held.shape
    p_size = columns // width
    shape = (z_count, sectors, p_size, width // (z_count * CORES), width)
    steps = sectors * sources // LEFT_TERMS
    return pl.pallas_call(
        functools.partial(left_kernel, z_count, p_size),
        in_specs=[
            pl.BlockSpec(memory_space=pltpu.SMEM),
            pl.BlockSpec(memory_space=pl.ANY),
            pl.BlockSpec(memory_space=pl.ANY),
        ],
        out_specs=[pl.BlockSpec(memory_space=pltpu.VMEM)] * 2,
        out_shape=[
            jax.ShapeDtypeStruct(shape, jnp.float32),
            jax.ShapeDtypeStruct(shape, jnp.bfloat16),
        ],
        scratch_shapes=[
            pltpu.VMEM((sectors, sources, width, width), jnp.bfloat16),
            pltpu.VMEM((sectors, sources, width, columns), jnp.bfloat16),
            pltpu.VMEM((width, columns), jnp.float32),
            pltpu.SemaphoreType.DMA((steps,)),
            pltpu.SemaphoreType.DMA((steps,)),
        ],
        compiler_params=pltpu.CompilerParams(vmem_limit_bytes=VMEM_LIMIT),
        name="left_terms",
    )(meta, left, held)


def join_kernel(keep_ref, take_ref, *outs):
    for shift, out in enumerate(outs):
        out[...] = (keep_ref[shift] + take_ref[shift].astype(jnp.float32)).astype(out.dtype)


def join_call(keep, take):
    z_count, shape = keep.shape[0], keep.shape[1:]
    return pl.pallas_call(
        join_kernel,
        in_specs=[pl.BlockSpec(memory_space=pltpu.VMEM)] * 2,
        out_specs=[pl.BlockSpec(memory_space=pltpu.VMEM)] * z_count,
        out_shape=[
            jax.ShapeDtypeStruct(shape, jnp.float32 if s == 0 else jnp.bfloat16)
            for s in range(z_count)
        ],
        compiler_params=pltpu.CompilerParams(vmem_limit_bytes=16 << 20),
        name="join_cores",
    )(keep, take)


def shards(wave, sector_dims, left_ops, right_ops, site_ops):
    z_count = lax.axis_size("z")
    op_at, z_at, core = lax.axis_index("op"), lax.axis_index("z"), lax.axis_index("core")
    sectors, width = wave.shape[0], wave.shape[1]

    left = lax.all_to_all(left_ops[:, 0], "op", split_axis=0, concat_axis=0, tiled=True)
    left = left.reshape(-1, sectors, width, width)

    sizes = lax.dynamic_slice_in_dim(sector_dims, op_at * sectors, sectors)
    mask = (lax.broadcasted_iota(jnp.int32, (sectors, width), 1) < sizes[:, None]).astype(
        jnp.float32
    )
    masked = wave.astype(jnp.float32) * mask[:, :, None, None] * mask[:, None, None, :]
    masked = masked.astype(jnp.bfloat16).transpose(0, 2, 1, 3)
    site = site_ops.reshape(site_ops.shape[0], -1)
    sec_at = z_at * CORES + core
    meta = jnp.stack([z_at, sec_at, jnp.int32(z_count * CORES)]).astype(jnp.int32)
    held = right_call(meta, site, masked, right_ops)

    keep, give = left_call(meta, left, held, z_count)
    parts = join_call(keep, lax.ppermute(give, "core", [(0, 1), (1, 0)]))
    total = parts[0]
    for shift in sorted(range(1, z_count), key=lambda s: -min(s, z_count - s)):
        ring = [(z, (z + shift) % z_count) for z in range(z_count)]
        total = total + lax.ppermute(parts[shift], "z", ring).astype(jnp.float32)

    rows = width // (z_count * CORES)
    row_mask = lax.dynamic_slice_in_dim(mask, sec_at * rows, rows, 1)
    share = total * row_mask[:, None, :, None] * mask[:, None, None, :]
    return share.astype(jnp.bfloat16).transpose(0, 2, 1, 3)


def solution(mesh):
    op_count, sec_count = mesh.shape["op"], mesh.shape["sec"]
    split = Mesh(
        mesh.devices.reshape(op_count, sec_count // CORES, CORES), ("op", "z", "core")
    )
    placed = (
        P("op", None, None, None),
        P(),
        P(None, ("op", "z", "core"), None, None),
        P("op", None, ("z", "core"), None, None),
        P(),
    )
    return jax.shard_map(
        shards, mesh=split, in_specs=placed,
        out_specs=P("op", ("z", "core"), None, None), check_vma=False,
    )
```

```python
import functools

import jax
import jax.numpy as jnp
from jax import lax
from jax.experimental import pallas as pl
from jax.experimental.pallas import tpu as pltpu
from jax.sharding import Mesh, PartitionSpec as P

CORES = 2
GROUP = 2
ROWS = 16
LEFT_TERMS = 2
DIRECT = 4
VMEM_LIMIT = 48 << 20


def right_kernel(group, meta, site_ref, wave_ref, own_ref, other_ref, held_ref, first):
    step = pl.program_id(0)
    core, z_at, sec_count = meta[0], meta[1], meta[2]
    p_size, width = wave_ref.shape[0], wave_ref.shape[1]
    waves = wave_ref[...].reshape(p_size * width, width)
    for at in range(group):
        source = step * group + at
        for slot in range(CORES):
            side = core if slot == 0 else 1 - core
            term = source * sec_count + z_at * CORES + side
            buf = (at * CORES + slot) % 2
            first[buf] = lax.dot_general(
                waves, (own_ref if slot == 0 else other_ref)[0, at, 0],
                (((1,), (1,)), ((), ())), preferred_element_type=jnp.float32,
            )
            scale = [[site_ref[term, q * p_size + p] for p in range(p_size)] for q in range(p_size)]
            place = at * CORES + side
            for low in range(0, width, ROWS):
                parts = [first[buf, p * width + low : p * width + low + ROWS] for p in range(p_size)]
                for q in range(p_size):
                    second = parts[0] * scale[q][0]
                    for p in range(1, p_size):
                        second = second + parts[p] * scale[q][p]
                    held_ref[place, low : low + ROWS, q * width : (q + 1) * width] = second.astype(
                        jnp.bfloat16
                    )


def right_call(meta, site, wave, own, other):
    sources, width = own.shape[1] - DIRECT, own.shape[-1]
    p_size = wave.shape[0]
    right_spec = pl.BlockSpec(
        (1, GROUP, 1, width, width), lambda step, meta: (meta[0], step, 0, 0, 0)
    )
    return pl.pallas_call(
        functools.partial(right_kernel, GROUP),
        grid_spec=pltpu.PrefetchScalarGridSpec(
            num_scalar_prefetch=1,
            grid=(sources // GROUP,),
            in_specs=[
                pl.BlockSpec(memory_space=pltpu.SMEM),
                pl.BlockSpec((p_size, width, width), lambda step, meta: (0, 0, 0)),
                right_spec,
                right_spec,
            ],
            out_specs=pl.BlockSpec(
                (GROUP * CORES, width, p_size * width), lambda step, meta: (step, 0, 0)
            ),
            scratch_shapes=[pltpu.VMEM((2, p_size * width, width), jnp.float32)],
        ),
        out_shape=jax.ShapeDtypeStruct((sources * CORES, width, p_size * width), jnp.bfloat16),
        compiler_params=pltpu.CompilerParams(vmem_limit_bytes=VMEM_LIMIT),
        name="right_terms",
    )(meta, site, wave, own, other)


def left_kernel(z_count, p_size, meta, site_ref, left_hbm, held_hbm, wave_hbm, own_hbm, other_hbm, *refs):
    outs = refs[:z_count]
    left, held, wave, rights, first, mixed, total, left_sem, held_sem, side_sem = refs[z_count:]
    z_at, core, sec_count = meta[1], meta[0], meta[2]
    terms, width = left.shape[0], left.shape[1]
    sources = terms // CORES
    ready = sources - DIRECT

    def left_copy(slot):
        span = pl.ds(slot * LEFT_TERMS, LEFT_TERMS)
        return pltpu.make_async_copy(left_hbm.at[span], left.at[span], left_sem.at[slot])

    def held_copy(slot):
        span = pl.ds(slot * LEFT_TERMS, LEFT_TERMS)
        return pltpu.make_async_copy(held_hbm.at[span], held.at[span], held_sem.at[slot])

    held_slots = ready * CORES // LEFT_TERMS
    slots = terms // LEFT_TERMS
    side_copies = [
        pltpu.make_async_copy(wave_hbm, wave, side_sem.at[0]),
        pltpu.make_async_copy(
            own_hbm.at[core, pl.ds(ready, DIRECT), 0], rights.at[0], side_sem.at[1]
        ),
        pltpu.make_async_copy(
            other_hbm.at[core, pl.ds(ready, DIRECT), 0], rights.at[1], side_sem.at[2]
        ),
    ]
    late = [left_copy(slot) for slot in range(held_slots, slots)]
    side_copies[0].start()
    for copy in late:
        copy.start()
    for copy in side_copies[1:]:
        copy.start()
    pairs = [(left_copy(slot), held_copy(slot)) for slot in range(held_slots)]
    for pair in pairs:
        for copy in pair:
            copy.start()

    side_copies[0].wait()
    for copy in late:
        copy.wait()
    for copy in side_copies[1:]:
        copy.wait()
    for at in range(DIRECT):
        for slot in range(CORES):
            side = core if slot == 0 else 1 - core
            source = ready + at
            term = source * sec_count + z_at * CORES + side
            for p in range(p_size):
                first[slot, p] = jnp.dot(
                    left[source * CORES + side], wave[p], preferred_element_type=jnp.float32
                )
            scale = [[site_ref[term, q * p_size + p] for p in range(p_size)] for q in range(p_size)]
            for low in range(0, width, ROWS):
                parts = [first[slot, p, low : low + ROWS] for p in range(p_size)]
                for q in range(p_size):
                    second = parts[0] * scale[q][0]
                    for p in range(1, p_size):
                        second = second + parts[p] * scale[q][p]
                    mixed[at % 2, q, low : low + ROWS, slot * width : (slot + 1) * width] = (
                        second.astype(jnp.bfloat16)
                    )
        right = jnp.concatenate([rights[slot, at] for slot in range(CORES)], axis=1)
        for q in range(p_size):
            product = lax.dot_general(
                mixed[at % 2, q], right, (((1,), (1,)), ((), ())),
                preferred_element_type=jnp.float32,
            )
            columns = slice(q * width, (q + 1) * width)
            if at == 0:
                total[:, columns] = product
            else:
                total[:, columns] += product

    for slot, pair in enumerate(pairs):
        for copy in pair:
            copy.wait()
        add = None
        for at in range(slot * LEFT_TERMS, (slot + 1) * LEFT_TERMS):
            product = jnp.dot(left[at], held[at], preferred_element_type=jnp.float32)
            add = product if add is None else add + product
        total[...] += add

    rows = width // z_count
    for shift in range(z_count):
        start = pl.multiple_of(lax.rem(z_at + shift, z_count) * rows, rows)
        block = total[pl.ds(start, rows), :]
        for q in range(p_size):
            outs[shift][q] = block[:, q * width : (q + 1) * width].astype(outs[shift].dtype)


def left_call(meta, site, left, held, wave, own, other, z_count):
    terms, width = left.shape[0], left.shape[1]
    ready, columns = held.shape[0], held.shape[2]
    p_size = columns // width
    rows = width // z_count
    return pl.pallas_call(
        functools.partial(left_kernel, z_count, p_size),
        in_specs=[pl.BlockSpec(memory_space=pltpu.SMEM)] * 2
        + [pl.BlockSpec(memory_space=pl.ANY)] * 5,
        out_specs=[pl.BlockSpec(memory_space=pltpu.VMEM)] * z_count,
        out_shape=[
            jax.ShapeDtypeStruct((p_size, rows, width), jnp.float32 if s == 0 else jnp.bfloat16)
            for s in range(z_count)
        ],
        scratch_shapes=[
            pltpu.VMEM((terms, width, width), jnp.bfloat16),
            pltpu.VMEM((ready, width, columns), jnp.bfloat16),
            pltpu.VMEM((p_size, width, width), jnp.bfloat16),
            pltpu.VMEM((CORES, DIRECT, width, width), jnp.bfloat16),
            pltpu.VMEM((CORES, p_size, width, width), jnp.float32),
            pltpu.VMEM((2, p_size, width, CORES * width), jnp.bfloat16),
            pltpu.VMEM((width, columns), jnp.float32),
            pltpu.SemaphoreType.DMA((terms // LEFT_TERMS,)),
            pltpu.SemaphoreType.DMA((ready // LEFT_TERMS,)),
            pltpu.SemaphoreType.DMA((3,)),
        ],
        compiler_params=pltpu.CompilerParams(vmem_limit_bytes=VMEM_LIMIT),
        name="left_terms",
    )(meta, site, left, held, wave, own, other)


def shards(wave, sector_dims, left_ops, right_ops, site_ops):
    z_count = lax.axis_size("z")
    op_at, z_at, core = lax.axis_index("op"), lax.axis_index("z"), lax.axis_index("core")
    width, p_size = wave.shape[1], wave.shape[2]
    swap = [(0, 1), (1, 0)]

    other = lax.ppermute(right_ops, "core", swap)
    left = lax.all_to_all(left_ops[:, 0], ("op", "core"), split_axis=0, concat_axis=0, tiled=True)

    size = lax.dynamic_slice_in_dim(sector_dims, op_at * CORES + core, 1)
    mask = (lax.iota(jnp.int32, width) < size).astype(jnp.float32)
    block = lax.dynamic_index_in_dim(wave, core, 0, keepdims=False)
    masked = block.astype(jnp.float32) * mask[:, None, None] * mask[None, None, :]
    masked = masked.astype(jnp.bfloat16).transpose(1, 0, 2)

    meta = jnp.stack([core, z_at, jnp.int32(z_count * CORES)]).astype(jnp.int32)
    site = site_ops.reshape(site_ops.shape[0], -1)
    held = right_call(meta, site, masked, right_ops, other)
    parts = left_call(meta, site, left, held, masked, right_ops, other, z_count)

    total = parts[0]
    for shift in sorted(range(1, z_count), key=lambda s: -min(s, z_count - s)):
        ring = [(z, (z + shift) % z_count) for z in range(z_count)]
        total = total + lax.ppermute(parts[shift], "z", ring).astype(jnp.float32)

    rows = width // z_count
    row_mask = lax.dynamic_slice_in_dim(mask, z_at * rows, rows)
    share = (total * row_mask[None, :, None] * mask[None, None, :]).astype(jnp.bfloat16)
    share = share.transpose(1, 0, 2).reshape(CORES, rows // CORES, p_size, width)
    keep = lax.dynamic_index_in_dim(share, core, 0, keepdims=False)
    give = lax.dynamic_index_in_dim(share, 1 - core, 0, keepdims=False)
    take = lax.ppermute(give, "core", swap)
    first = core == 0
    return jnp.stack([jnp.where(first, keep, take), jnp.where(first, take, keep)])


def solution(mesh):
    op_count, sec_count = mesh.shape["op"], mesh.shape["sec"]
    split = Mesh(
        mesh.devices.reshape(op_count, sec_count // CORES, CORES), ("op", "z", "core")
    )
    placed = (
        P("op", None, None, None),
        P(),
        P(None, ("op", "z", "core"), None, None),
        P("op", None, ("z", "core"), None, None),
        P(),
    )
    return jax.shard_map(
        shards, mesh=split, in_specs=placed,
        out_specs=P("op", ("z", "core"), None, None), check_vma=False,
    )
```

```python
import functools

import jax
import jax.numpy as jnp
from jax import lax
from jax.experimental import pallas as pl
from jax.experimental.pallas import tpu as pltpu
from jax.sharding import Mesh, PartitionSpec as P

CORES = 2
GROUP = 2
ROWS = 16
LEFT_TERMS = 2
KEPT = 2
VMEM_LIMIT = 52 << 20


def right_kernel(group, base, meta, site_ref, wave_ref, own_ref, other_ref, held_ref, first):
    step = pl.program_id(0)
    core, z_at, sec_count = meta[0], meta[1], meta[2]
    p_size, width = wave_ref.shape[0], wave_ref.shape[1]
    waves = wave_ref[...].reshape(p_size * width, width)
    for at in range(group):
        source = base + step * group + at
        for slot in range(CORES):
            side = core if slot == 0 else 1 - core
            term = source * sec_count + z_at * CORES + side
            buf = (at * CORES + slot) % 2
            first[buf] = lax.dot_general(
                waves, (own_ref if slot == 0 else other_ref)[0, at, 0],
                (((1,), (1,)), ((), ())), preferred_element_type=jnp.float32,
            )
            scale = [[site_ref[term, q * p_size + p] for p in range(p_size)] for q in range(p_size)]
            place = at * CORES + side
            for low in range(0, width, ROWS):
                parts = [first[buf, p * width + low : p * width + low + ROWS] for p in range(p_size)]
                for q in range(p_size):
                    second = parts[0] * scale[q][0]
                    for p in range(1, p_size):
                        second = second + parts[p] * scale[q][p]
                    held_ref[place, low : low + ROWS, q * width : (q + 1) * width] = second.astype(
                        jnp.bfloat16
                    )


def right_call(meta, site, wave, own, other, base, sources):
    width = own.shape[-1]
    p_size = wave.shape[0]
    right_spec = pl.BlockSpec(
        (1, GROUP, 1, width, width), lambda step, meta: (meta[0], base // GROUP + step, 0, 0, 0)
    )
    return pl.pallas_call(
        functools.partial(right_kernel, GROUP, base),
        grid_spec=pltpu.PrefetchScalarGridSpec(
            num_scalar_prefetch=1,
            grid=(sources // GROUP,),
            in_specs=[
                pl.BlockSpec(memory_space=pltpu.SMEM),
                pl.BlockSpec((p_size, width, width), lambda step, meta: (0, 0, 0)),
                right_spec,
                right_spec,
            ],
            out_specs=pl.BlockSpec(
                (GROUP * CORES, width, p_size * width), lambda step, meta: (step, 0, 0)
            ),
            scratch_shapes=[pltpu.VMEM((2, p_size * width, width), jnp.float32)],
        ),
        out_shape=jax.ShapeDtypeStruct((sources * CORES, width, p_size * width), jnp.bfloat16),
        compiler_params=pltpu.CompilerParams(vmem_limit_bytes=VMEM_LIMIT),
        name="right_terms",
    )(meta, site, wave, own, other)


def left_kernel(z_count, p_size, meta, left_hbm, kept_ref, held_hbm, *refs):
    outs = refs[:z_count]
    left, held, total, left_sem, held_sem = refs[z_count:]
    z_at = meta[1]
    terms, width = left.shape[0], left.shape[1]
    kept = kept_ref.shape[0]
    copies = []
    for at in range(0, terms, LEFT_TERMS):
        span = pl.ds(at, LEFT_TERMS)
        slot = at // LEFT_TERMS
        now = [pltpu.make_async_copy(left_hbm.at[span], left.at[span], left_sem.at[slot])]
        if at >= kept:
            span = pl.ds(at - kept, LEFT_TERMS)
            now.append(pltpu.make_async_copy(held_hbm.at[span], held.at[span], held_sem.at[slot]))
        for copy in now:
            copy.start()
        copies.append(now)

    for slot, now in enumerate(copies):
        for copy in now:
            copy.wait()
        add = None
        for at in range(slot * LEFT_TERMS, (slot + 1) * LEFT_TERMS):
            right = kept_ref[at] if at < kept else held[at - kept]
            product = jnp.dot(left[at], right, preferred_element_type=jnp.float32)
            add = product if add is None else add + product
        if slot == 0:
            total[...] = add
        else:
            total[...] += add

    rows = width // z_count
    for shift in range(z_count):
        start = pl.multiple_of(lax.rem(z_at + shift, z_count) * rows, rows)
        block = total[pl.ds(start, rows), :]
        for q in range(p_size):
            outs[shift][q] = block[:, q * width : (q + 1) * width].astype(outs[shift].dtype)


def left_call(meta, left, kept, held, z_count):
    terms, width = left.shape[:2]
    columns = held.shape[2]
    p_size = columns // width
    rows = width // z_count
    return pl.pallas_call(
        functools.partial(left_kernel, z_count, p_size),
        in_specs=[
            pl.BlockSpec(memory_space=pltpu.SMEM),
            pl.BlockSpec(memory_space=pl.ANY),
            pl.BlockSpec(memory_space=pltpu.VMEM),
            pl.BlockSpec(memory_space=pl.ANY),
        ],
        out_specs=[pl.BlockSpec(memory_space=pltpu.VMEM)] * z_count,
        out_shape=[
            jax.ShapeDtypeStruct((p_size, rows, width), jnp.float32 if s == 0 else jnp.bfloat16)
            for s in range(z_count)
        ],
        scratch_shapes=[
            pltpu.VMEM((terms, width, width), jnp.bfloat16),
            pltpu.VMEM(held.shape, jnp.bfloat16),
            pltpu.VMEM((width, columns), jnp.float32),
            pltpu.SemaphoreType.DMA((terms // LEFT_TERMS,)),
            pltpu.SemaphoreType.DMA((terms // LEFT_TERMS,)),
        ],
        compiler_params=pltpu.CompilerParams(vmem_limit_bytes=VMEM_LIMIT),
        name="left_terms",
    )(meta, left, kept, held)


def shards(wave, sector_dims, left_ops, right_ops, site_ops):
    z_count = lax.axis_size("z")
    op_at, z_at, core = lax.axis_index("op"), lax.axis_index("z"), lax.axis_index("core")
    width, p_size = wave.shape[1], wave.shape[2]
    swap = [(0, 1), (1, 0)]

    other = lax.ppermute(right_ops, "core", swap)
    left = lax.all_to_all(left_ops[:, 0], ("op", "core"), split_axis=0, concat_axis=0, tiled=True)

    size = lax.dynamic_slice_in_dim(sector_dims, op_at * CORES + core, 1)
    mask = (lax.iota(jnp.int32, width) < size).astype(jnp.float32)
    block = lax.dynamic_index_in_dim(wave, core, 0, keepdims=False)
    masked = block.astype(jnp.float32) * mask[:, None, None] * mask[None, None, :]
    masked = masked.astype(jnp.bfloat16).transpose(1, 0, 2)

    meta = jnp.stack([core, z_at, jnp.int32(z_count * CORES)]).astype(jnp.int32)
    site = site_ops.reshape(site_ops.shape[0], -1)
    sources = right_ops.shape[1]
    held = right_call(meta, site, masked, right_ops, other, KEPT, sources - KEPT)
    kept = right_call(meta, site, masked, right_ops, other, 0, KEPT)
    parts = left_call(meta, left, kept, held, z_count)

    total = parts[0]
    for shift in sorted(range(1, z_count), key=lambda s: -min(s, z_count - s)):
        ring = [(z, (z + shift) % z_count) for z in range(z_count)]
        total = total + lax.ppermute(parts[shift], "z", ring).astype(jnp.float32)

    rows = width // z_count
    row_mask = lax.dynamic_slice_in_dim(mask, z_at * rows, rows)
    share = (total * row_mask[None, :, None] * mask[None, None, :]).astype(jnp.bfloat16)
    share = share.transpose(1, 0, 2).reshape(CORES, rows // CORES, p_size, width)
    keep = lax.dynamic_index_in_dim(share, core, 0, keepdims=False)
    give = lax.dynamic_index_in_dim(share, 1 - core, 0, keepdims=False)
    take = lax.ppermute(give, "core", swap)
    first = core == 0
    return jnp.stack([jnp.where(first, keep, take), jnp.where(first, take, keep)])


def solution(mesh):
    op_count, sec_count = mesh.shape["op"], mesh.shape["sec"]
    split = Mesh(
        mesh.devices.reshape(op_count, sec_count // CORES, CORES), ("op", "z", "core")
    )
    placed = (
        P("op", None, None, None),
        P(),
        P(None, ("op", "z", "core"), None, None),
        P("op", None, ("z", "core"), None, None),
        P(),
    )
    return jax.shard_map(
        shards, mesh=split, in_specs=placed,
        out_specs=P("op", ("z", "core"), None, None), check_vma=False,
    )
```

```python
import functools

import jax
import jax.numpy as jnp
from jax import lax
from jax.experimental import pallas as pl
from jax.experimental.pallas import tpu as pltpu
from jax.sharding import Mesh, PartitionSpec as P

CORES = 2
GROUP = 2
ROWS = 16
LEFT_TERMS = 2
KEPT = 2
VMEM_LIMIT = 32 << 20
TAIL_VMEM = 48 << 20


def right_kernel(group, base, meta, site_ref, wave_ref, own_ref, other_ref, held_ref, first):
    step = pl.program_id(0)
    core, z_at, sec_count = meta[0], meta[1], meta[2]
    p_size, width = wave_ref.shape[0], wave_ref.shape[1]
    waves = wave_ref[...].reshape(p_size * width, width)
    for at in range(group):
        source = base + step * group + at
        for slot in range(CORES):
            side = core if slot == 0 else 1 - core
            term = source * sec_count + z_at * CORES + side
            buf = (at * CORES + slot) % 2
            first[buf] = lax.dot_general(
                waves, (own_ref if slot == 0 else other_ref)[0, at, 0],
                (((1,), (1,)), ((), ())), preferred_element_type=jnp.float32,
            )
            scale = [[site_ref[term, q * p_size + p] for p in range(p_size)] for q in range(p_size)]
            place = at * CORES + side
            for low in range(0, width, ROWS):
                parts = [first[buf, p * width + low : p * width + low + ROWS] for p in range(p_size)]
                for q in range(p_size):
                    second = parts[0] * scale[q][0]
                    for p in range(1, p_size):
                        second = second + parts[p] * scale[q][p]
                    held_ref[place, low : low + ROWS, q * width : (q + 1) * width] = second.astype(
                        jnp.bfloat16
                    )


def right_call(meta, site, wave, own, other, base, sources):
    width = own.shape[-1]
    p_size = wave.shape[0]
    right_spec = pl.BlockSpec(
        (1, GROUP, 1, width, width), lambda step, meta: (meta[0], base // GROUP + step, 0, 0, 0)
    )
    return pl.pallas_call(
        functools.partial(right_kernel, GROUP, base),
        grid_spec=pltpu.PrefetchScalarGridSpec(
            num_scalar_prefetch=1,
            grid=(sources // GROUP,),
            in_specs=[
                pl.BlockSpec(memory_space=pltpu.SMEM),
                pl.BlockSpec((p_size, width, width), lambda step, meta: (0, 0, 0)),
                right_spec,
                right_spec,
            ],
            out_specs=pl.BlockSpec(
                (GROUP * CORES, width, p_size * width), lambda step, meta: (step, 0, 0)
            ),
            scratch_shapes=[pltpu.VMEM((2, p_size * width, width), jnp.float32)],
        ),
        out_shape=jax.ShapeDtypeStruct((sources * CORES, width, p_size * width), jnp.bfloat16),
        compiler_params=pltpu.CompilerParams(vmem_limit_bytes=VMEM_LIMIT),
        name="right_terms",
    )(meta, site, wave, own, other)


def left_kernel(z_count, p_size, meta, left_hbm, kept_ref, held_hbm, *refs):
    outs = refs[:z_count]
    left, held, total, left_sem, held_sem = refs[z_count:]
    z_at = meta[1]
    terms, width = left.shape[0], left.shape[1]
    kept = kept_ref.shape[0]
    copies = []
    for at in range(0, terms, LEFT_TERMS):
        span = pl.ds(at, LEFT_TERMS)
        slot = at // LEFT_TERMS
        now = [pltpu.make_async_copy(left_hbm.at[span], left.at[span], left_sem.at[slot])]
        if at >= kept:
            span = pl.ds(at - kept, LEFT_TERMS)
            now.append(pltpu.make_async_copy(held_hbm.at[span], held.at[span], held_sem.at[slot]))
        for copy in now:
            copy.start()
        copies.append(now)

    for slot, now in enumerate(copies):
        for copy in now:
            copy.wait()
        add = None
        for at in range(slot * LEFT_TERMS, (slot + 1) * LEFT_TERMS):
            right = kept_ref[at] if at < kept else held[at - kept]
            product = jnp.dot(left[at], right, preferred_element_type=jnp.float32)
            add = product if add is None else add + product
        if slot == 0:
            total[...] = add
        else:
            total[...] += add

    rows = width // z_count
    for shift in range(z_count):
        start = pl.multiple_of(lax.rem(z_at + shift, z_count) * rows, rows)
        block = total[pl.ds(start, rows), :]
        for q in range(p_size):
            outs[shift][q] = block[:, q * width : (q + 1) * width].astype(outs[shift].dtype)


def left_call(meta, left, kept, held, z_count):
    terms, width = left.shape[:2]
    columns = held.shape[2]
    p_size = columns // width
    rows = width // z_count
    return pl.pallas_call(
        functools.partial(left_kernel, z_count, p_size),
        in_specs=[
            pl.BlockSpec(memory_space=pltpu.SMEM),
            pl.BlockSpec(memory_space=pl.ANY),
            pl.BlockSpec(memory_space=pltpu.VMEM),
            pl.BlockSpec(memory_space=pl.ANY),
        ],
        out_specs=[pl.BlockSpec(memory_space=pltpu.VMEM)] * z_count,
        out_shape=[
            jax.ShapeDtypeStruct((p_size, rows, width), jnp.float32 if s == 0 else jnp.bfloat16)
            for s in range(z_count)
        ],
        scratch_shapes=[
            pltpu.VMEM((terms, width, width), jnp.bfloat16),
            pltpu.VMEM(held.shape, jnp.bfloat16),
            pltpu.VMEM((width, columns), jnp.float32),
            pltpu.SemaphoreType.DMA((terms // LEFT_TERMS,)),
            pltpu.SemaphoreType.DMA((terms // LEFT_TERMS,)),
        ],
        compiler_params=pltpu.CompilerParams(vmem_limit_bytes=TAIL_VMEM),
        name="left_terms",
    )(meta, left, kept, held)


def shards(wave, sector_dims, left_ops, right_ops, site_ops):
    z_count = lax.axis_size("z")
    op_at, z_at, core = lax.axis_index("op"), lax.axis_index("z"), lax.axis_index("core")
    width, p_size = wave.shape[1], wave.shape[2]
    swap = [(0, 1), (1, 0)]

    other = lax.ppermute(right_ops, "core", swap)
    left = lax.all_to_all(left_ops[:, 0], ("op", "core"), split_axis=0, concat_axis=0, tiled=True)

    size = lax.dynamic_slice_in_dim(sector_dims, op_at * CORES + core, 1)
    mask = (lax.iota(jnp.int32, width) < size).astype(jnp.float32)
    block = lax.dynamic_index_in_dim(wave, core, 0, keepdims=False)
    masked = block.astype(jnp.float32) * mask[:, None, None] * mask[None, None, :]
    masked = masked.astype(jnp.bfloat16).transpose(1, 0, 2)

    meta = jnp.stack([core, z_at, jnp.int32(z_count * CORES)]).astype(jnp.int32)
    site = site_ops.reshape(site_ops.shape[0], -1)
    sources = right_ops.shape[1]
    held = right_call(meta, site, masked, right_ops, other, KEPT, sources - KEPT)
    kept = right_call(meta, site, masked, right_ops, other, 0, KEPT)
    parts = left_call(meta, left, kept, held, z_count)

    total = parts[0]
    for shift in sorted(range(1, z_count), key=lambda s: -min(s, z_count - s)):
        ring = [(z, (z + shift) % z_count) for z in range(z_count)]
        total = total + lax.ppermute(parts[shift], "z", ring).astype(jnp.float32)

    rows = width // z_count
    row_mask = lax.dynamic_slice_in_dim(mask, z_at * rows, rows)
    share = (total * row_mask[None, :, None] * mask[None, None, :]).astype(jnp.bfloat16)
    share = share.transpose(1, 0, 2).reshape(CORES, rows // CORES, p_size, width)
    keep = lax.dynamic_index_in_dim(share, core, 0, keepdims=False)
    give = lax.dynamic_index_in_dim(share, 1 - core, 0, keepdims=False)
    take = lax.ppermute(give, "core", swap)
    first = core == 0
    return jnp.stack([jnp.where(first, keep, take), jnp.where(first, take, keep)])


def solution(mesh):
    op_count, sec_count = mesh.shape["op"], mesh.shape["sec"]
    split = Mesh(
        mesh.devices.reshape(op_count, sec_count // CORES, CORES), ("op", "z", "core")
    )
    placed = (
        P("op", None, None, None),
        P(),
        P(None, ("op", "z", "core"), None, None),
        P("op", None, ("z", "core"), None, None),
        P(),
    )
    return jax.shard_map(
        shards, mesh=split, in_specs=placed,
        out_specs=P("op", ("z", "core"), None, None), check_vma=False,
    )
```

```python
import functools

import jax
import jax.numpy as jnp
from jax import lax
from jax.experimental import pallas as pl
from jax.experimental.pallas import tpu as pltpu
from jax.sharding import Mesh, PartitionSpec as P

CORES = 2
GROUP = 2
ROWS = 16
LEFT_TERMS = 2
VMEM_LIMIT = 48 << 20


def right_kernel(group, meta, site_ref, wave_ref, own_ref, other_ref, held_ref, first):
    step = pl.program_id(0)
    core, z_at, sec_count = meta[0], meta[1], meta[2]
    p_size, width = wave_ref.shape[0], wave_ref.shape[1]
    waves = wave_ref[...].reshape(p_size * width, width)
    for at in range(group):
        source = step * group + at
        for slot in range(CORES):
            side = core if slot == 0 else 1 - core
            term = source * sec_count + z_at * CORES + side
            buf = (at * CORES + slot) % 2
            first[buf] = lax.dot_general(
                waves, (own_ref if slot == 0 else other_ref)[0, at, 0],
                (((1,), (1,)), ((), ())), preferred_element_type=jnp.float32,
            )
            scale = [[site_ref[term, q * p_size + p] for p in range(p_size)] for q in range(p_size)]
            place = at * CORES + side
            for low in range(0, width, ROWS):
                parts = [first[buf, p * width + low : p * width + low + ROWS] for p in range(p_size)]
                for q in range(p_size):
                    second = parts[0] * scale[q][0]
                    for p in range(1, p_size):
                        second = second + parts[p] * scale[q][p]
                    held_ref[place, low : low + ROWS, q * width : (q + 1) * width] = second.astype(
                        jnp.bfloat16
                    )


def right_call(meta, site, wave, own, other):
    sources, width = own.shape[1], own.shape[-1]
    p_size = wave.shape[0]
    right_spec = pl.BlockSpec(
        (1, GROUP, 1, width, width), lambda step, meta: (meta[0], step, 0, 0, 0)
    )
    return pl.pallas_call(
        functools.partial(right_kernel, GROUP),
        grid_spec=pltpu.PrefetchScalarGridSpec(
            num_scalar_prefetch=1,
            grid=(sources // GROUP,),
            in_specs=[
                pl.BlockSpec(memory_space=pltpu.SMEM),
                pl.BlockSpec((p_size, width, width), lambda step, meta: (0, 0, 0)),
                right_spec,
                right_spec,
            ],
            out_specs=pl.BlockSpec(
                (GROUP * CORES, width, p_size * width), lambda step, meta: (step, 0, 0)
            ),
            scratch_shapes=[pltpu.VMEM((2, p_size * width, width), jnp.float32)],
        ),
        out_shape=jax.ShapeDtypeStruct((sources * CORES, width, p_size * width), jnp.bfloat16),
        compiler_params=pltpu.CompilerParams(vmem_limit_bytes=VMEM_LIMIT),
        name="right_terms",
    )(meta, site, wave, own, other)


def near_shifts(z_count):
    return [shift for shift in range(z_count) if shift != z_count // 2]


def left_kernel(z_count, p_size, meta, left_hbm, held_hbm, *refs):
    *outs, left, held, total, left_sem, held_sem = refs
    z_at = meta[1]
    terms, width = left.shape[0], left.shape[1]
    copies = []
    for at in range(0, terms, LEFT_TERMS):
        span = pl.ds(at, LEFT_TERMS)
        slot = at // LEFT_TERMS
        pair = (
            pltpu.make_async_copy(left_hbm.at[span], left.at[span], left_sem.at[slot]),
            pltpu.make_async_copy(held_hbm.at[span], held.at[span], held_sem.at[slot]),
        )
        for copy in pair:
            copy.start()
        copies.append(pair)

    for slot, pair in enumerate(copies):
        for copy in pair:
            copy.wait()
        add = None
        for at in range(slot * LEFT_TERMS, (slot + 1) * LEFT_TERMS):
            product = jnp.dot(left[at], held[at], preferred_element_type=jnp.float32)
            add = product if add is None else add + product
        if slot == 0:
            total[...] = add
        else:
            total[...] += add

    rows = width // z_count
    half = rows // CORES
    core = meta[0]

    def cut(out, shift, low, count):
        start = lax.rem(z_at + shift, z_count) * rows + low
        block = total[pl.ds(pl.multiple_of(start, half), count), :]
        for q in range(p_size):
            out[q] = block[:, q * width : (q + 1) * width].astype(out.dtype)

    far_ref, keep_ref, give_ref, *near_refs = outs
    cut(far_ref, z_count // 2, 0, rows)
    cut(keep_ref, 0, core * half, half)
    for at, shift in enumerate(near_shifts(z_count)):
        cut(give_ref.at[at], shift, (1 - core) * half, half)
        if shift:
            cut(near_refs[at - 1], shift, core * half, half)


def left_call(meta, left, held, z_count):
    terms, width, columns = held.shape
    p_size = columns // width
    rows = width // z_count
    half = (p_size, rows // CORES, width)
    near = len(near_shifts(z_count))
    out_shape = [
        jax.ShapeDtypeStruct((p_size, rows, width), jnp.bfloat16),
        jax.ShapeDtypeStruct(half, jnp.float32),
        jax.ShapeDtypeStruct((near, *half), jnp.bfloat16),
    ] + [jax.ShapeDtypeStruct(half, jnp.bfloat16)] * (near - 1)
    return pl.pallas_call(
        functools.partial(left_kernel, z_count, p_size),
        in_specs=[
            pl.BlockSpec(memory_space=pltpu.SMEM),
            pl.BlockSpec(memory_space=pl.ANY),
            pl.BlockSpec(memory_space=pl.ANY),
        ],
        out_specs=[pl.BlockSpec(memory_space=pltpu.VMEM)] * len(out_shape),
        out_shape=out_shape,
        scratch_shapes=[
            pltpu.VMEM((terms, width, width), jnp.bfloat16),
            pltpu.VMEM((terms, width, columns), jnp.bfloat16),
            pltpu.VMEM((width, columns), jnp.float32),
            pltpu.SemaphoreType.DMA((terms // LEFT_TERMS,)),
            pltpu.SemaphoreType.DMA((terms // LEFT_TERMS,)),
        ],
        compiler_params=pltpu.CompilerParams(vmem_limit_bytes=VMEM_LIMIT),
        name="left_terms",
    )(meta, left, held)


def shards(wave, sector_dims, left_ops, right_ops, site_ops):
    z_count = lax.axis_size("z")
    op_at, z_at, core = lax.axis_index("op"), lax.axis_index("z"), lax.axis_index("core")
    width, p_size = wave.shape[1], wave.shape[2]
    swap = [(0, 1), (1, 0)]

    other = lax.ppermute(right_ops, "core", swap)
    left = lax.all_to_all(left_ops[:, 0], ("op", "core"), split_axis=0, concat_axis=0, tiled=True)

    size = lax.dynamic_slice_in_dim(sector_dims, op_at * CORES + core, 1)
    mask = (lax.iota(jnp.int32, width) < size).astype(jnp.float32)
    block = lax.dynamic_index_in_dim(wave, core, 0, keepdims=False)
    masked = block.astype(jnp.float32) * mask[:, None, None] * mask[None, None, :]
    masked = masked.astype(jnp.bfloat16).transpose(1, 0, 2)

    meta = jnp.stack([core, z_at, jnp.int32(z_count * CORES)]).astype(jnp.int32)
    site = site_ops.reshape(site_ops.shape[0], -1)
    held = right_call(meta, site, masked, right_ops, other)
    far, keep, give, *near = left_call(meta, left, held, z_count)

    def ring(block, shift):
        pairs = [(z, (z + shift) % z_count) for z in range(z_count)]
        return lax.ppermute(block, "z", pairs)

    far = ring(far, z_count // 2)
    take = lax.ppermute(give, "core", swap)
    mine, theirs = keep, take[0].astype(jnp.float32)
    for at, shift in enumerate(near_shifts(z_count)):
        if shift:
            both = ring(jnp.stack([near[at - 1], take[at]]), shift).astype(jnp.float32)
            mine, theirs = mine + both[0], theirs + both[1]
    half = keep.shape[1]
    far_mine = lax.dynamic_slice_in_dim(far, core * half, half, 1)
    far_give = lax.dynamic_slice_in_dim(far, (1 - core) * half, half, 1)
    mine = mine + far_mine.astype(jnp.float32)
    theirs = theirs + lax.ppermute(far_give, "core", swap).astype(jnp.float32)

    sizes = lax.dynamic_slice_in_dim(sector_dims, op_at * CORES, CORES)
    columns = lax.iota(jnp.int32, width)
    in_rows = (z_at * CORES + core) * half + lax.iota(jnp.int32, half)
    first = core == 0
    shares = []
    for sector, part in enumerate(
        (jnp.where(first, mine, theirs), jnp.where(first, theirs, mine))
    ):
        row_mask = (in_rows < sizes[sector]).astype(jnp.float32)
        column_mask = (columns < sizes[sector]).astype(jnp.float32)
        share = part * row_mask[None, :, None] * column_mask[None, None, :]
        shares.append(share.astype(jnp.bfloat16).transpose(1, 0, 2))
    return jnp.stack(shares)


def solution(mesh):
    op_count, sec_count = mesh.shape["op"], mesh.shape["sec"]
    split = Mesh(
        mesh.devices.reshape(op_count, sec_count // CORES, CORES), ("op", "z", "core")
    )
    placed = (
        P("op", None, None, None),
        P(),
        P(None, ("op", "z", "core"), None, None),
        P("op", None, ("z", "core"), None, None),
        P(),
    )
    return jax.shard_map(
        shards, mesh=split, in_specs=placed,
        out_specs=P("op", ("z", "core"), None, None), check_vma=False,
    )
```

```python
import functools

import jax
import jax.numpy as jnp
from jax import lax
from jax.experimental import pallas as pl
from jax.experimental.pallas import tpu as pltpu
from jax.sharding import Mesh, PartitionSpec as P

CORES = 2
GROUP = 2
ROWS = 16
LEFT_TERMS = 2
VMEM_LIMIT = 48 << 20


def right_kernel(group, meta, site_ref, wave_ref, own_ref, other_ref, held_ref, first):
    step = pl.program_id(0)
    core, z_at, sec_count = meta[0], meta[1], meta[2]
    p_size, width = wave_ref.shape[0], wave_ref.shape[1]
    waves = wave_ref[...].reshape(p_size * width, width)
    for at in range(group):
        source = step * group + at
        for slot in range(CORES):
            side = core if slot == 0 else 1 - core
            term = source * sec_count + z_at * CORES + side
            buf = (at * CORES + slot) % 2
            first[buf] = lax.dot_general(
                waves, (own_ref if slot == 0 else other_ref)[0, at, 0],
                (((1,), (1,)), ((), ())), preferred_element_type=jnp.float32,
            )
            scale = [[site_ref[term, q * p_size + p] for p in range(p_size)] for q in range(p_size)]
            place = at * CORES + side
            for low in range(0, width, ROWS):
                parts = [first[buf, p * width + low : p * width + low + ROWS] for p in range(p_size)]
                for q in range(p_size):
                    second = parts[0] * scale[q][0]
                    for p in range(1, p_size):
                        second = second + parts[p] * scale[q][p]
                    held_ref[place, low : low + ROWS, q * width : (q + 1) * width] = second.astype(
                        jnp.bfloat16
                    )


def right_call(meta, site, wave, own, other):
    sources, width = own.shape[1], own.shape[-1]
    p_size = wave.shape[0]
    right_spec = pl.BlockSpec(
        (1, GROUP, 1, width, width), lambda step, meta: (meta[0], step, 0, 0, 0)
    )
    return pl.pallas_call(
        functools.partial(right_kernel, GROUP),
        grid_spec=pltpu.PrefetchScalarGridSpec(
            num_scalar_prefetch=1,
            grid=(sources // GROUP,),
            in_specs=[
                pl.BlockSpec(memory_space=pltpu.SMEM),
                pl.BlockSpec((p_size, width, width), lambda step, meta: (0, 0, 0)),
                right_spec,
                right_spec,
            ],
            out_specs=pl.BlockSpec(
                (GROUP * CORES, width, p_size * width), lambda step, meta: (step, 0, 0)
            ),
            scratch_shapes=[pltpu.VMEM((2, p_size * width, width), jnp.float32)],
        ),
        out_shape=jax.ShapeDtypeStruct((sources * CORES, width, p_size * width), jnp.bfloat16),
        compiler_params=pltpu.CompilerParams(vmem_limit_bytes=VMEM_LIMIT),
        name="right_terms",
    )(meta, site, wave, own, other)


def near_shifts(z_count):
    return [shift for shift in range(z_count) if shift != z_count // 2]


def left_kernel(z_count, p_size, meta, left_hbm, held_hbm, *refs):
    *outs, left, held, total, left_sem, held_sem = refs
    z_at = meta[1]
    terms, width = left.shape[0], left.shape[1]
    copies = []
    for at in range(0, terms, LEFT_TERMS):
        span = pl.ds(at, LEFT_TERMS)
        slot = at // LEFT_TERMS
        pair = (
            pltpu.make_async_copy(left_hbm.at[span], left.at[span], left_sem.at[slot]),
            pltpu.make_async_copy(held_hbm.at[span], held.at[span], held_sem.at[slot]),
        )
        for copy in pair:
            copy.start()
        copies.append(pair)

    for slot, pair in enumerate(copies):
        for copy in pair:
            copy.wait()
        add = None
        for at in range(slot * LEFT_TERMS, (slot + 1) * LEFT_TERMS):
            product = jnp.dot(left[at], held[at], preferred_element_type=jnp.float32)
            add = product if add is None else add + product
        if slot == 0:
            total[...] = add
        else:
            total[...] += add

    rows = width // z_count
    half = rows // CORES
    core = meta[0]

    def cut(out, shift, low, count):
        start = lax.rem(z_at + shift, z_count) * rows + low
        block = total[pl.ds(pl.multiple_of(start, half), count), :]
        for q in range(p_size):
            out[q] = block[:, q * width : (q + 1) * width].astype(out.dtype)

    far_ref, keep_ref, give_ref, *near_refs = outs
    cut(far_ref, z_count // 2, 0, rows)
    cut(keep_ref, 0, core * half, half)
    for at, shift in enumerate(near_shifts(z_count)):
        cut(give_ref.at[at], shift, (1 - core) * half, half)
        if shift:
            cut(near_refs[at - 1], shift, core * half, half)


def left_call(meta, left, held, z_count):
    terms, width, columns = held.shape
    p_size = columns // width
    rows = width // z_count
    half = (p_size, rows // CORES, width)
    near = len(near_shifts(z_count))
    out_shape = [
        jax.ShapeDtypeStruct((p_size, rows, width), jnp.bfloat16),
        jax.ShapeDtypeStruct(half, jnp.float32),
        jax.ShapeDtypeStruct((near, *half), jnp.bfloat16),
    ] + [jax.ShapeDtypeStruct(half, jnp.bfloat16)] * (near - 1)
    return pl.pallas_call(
        functools.partial(left_kernel, z_count, p_size),
        in_specs=[
            pl.BlockSpec(memory_space=pltpu.SMEM),
            pl.BlockSpec(memory_space=pl.ANY),
            pl.BlockSpec(memory_space=pl.ANY),
        ],
        out_specs=[pl.BlockSpec(memory_space=pltpu.VMEM)] * len(out_shape),
        out_shape=out_shape,
        scratch_shapes=[
            pltpu.VMEM((terms, width, width), jnp.bfloat16),
            pltpu.VMEM((terms, width, columns), jnp.bfloat16),
            pltpu.VMEM((width, columns), jnp.float32),
            pltpu.SemaphoreType.DMA((terms // LEFT_TERMS,)),
            pltpu.SemaphoreType.DMA((terms // LEFT_TERMS,)),
        ],
        compiler_params=pltpu.CompilerParams(vmem_limit_bytes=VMEM_LIMIT),
        name="left_terms",
    )(meta, left, held)


def shards(wave, sector_dims, left_ops, right_ops, site_ops):
    z_count = lax.axis_size("z")
    op_at, z_at, core = lax.axis_index("op"), lax.axis_index("z"), lax.axis_index("core")
    width, p_size = wave.shape[1], wave.shape[2]
    swap = [(0, 1), (1, 0)]

    other = lax.ppermute(right_ops, "core", swap)
    left = lax.all_to_all(left_ops[:, 0], ("op", "core"), split_axis=0, concat_axis=0, tiled=True)

    sizes = lax.dynamic_slice_in_dim(sector_dims, op_at * CORES, CORES)
    masks = (lax.broadcasted_iota(jnp.int32, (CORES, width), 1) < sizes[:, None]).astype(
        jnp.float32
    )
    mask = lax.dynamic_index_in_dim(masks, core, 0, keepdims=False)
    block = lax.dynamic_index_in_dim(wave, core, 0, keepdims=False)
    masked = block.astype(jnp.float32) * mask[:, None, None] * mask[None, None, :]
    masked = masked.astype(jnp.bfloat16).transpose(1, 0, 2)

    meta = jnp.stack([core, z_at, jnp.int32(z_count * CORES)]).astype(jnp.int32)
    site = site_ops.reshape(site_ops.shape[0], -1)
    held = right_call(meta, site, masked, right_ops, other)
    far, keep, give, *near = left_call(meta, left, held, z_count)

    def ring(block, shift):
        pairs = [(z, (z + shift) % z_count) for z in range(z_count)]
        return lax.ppermute(block, "z", pairs)

    far = ring(far, z_count // 2)
    take = lax.ppermute(give, "core", swap)
    mine, theirs = keep, take[0].astype(jnp.float32)
    for at, shift in enumerate(near_shifts(z_count)):
        if shift:
            both = ring(jnp.stack([near[at - 1], take[at]]), shift).astype(jnp.float32)
            mine, theirs = mine + both[0], theirs + both[1]
    half = keep.shape[1]
    far_mine = lax.dynamic_slice_in_dim(far, core * half, half, 1)
    far_give = lax.dynamic_slice_in_dim(far, (1 - core) * half, half, 1)
    mine = mine + far_mine.astype(jnp.float32)
    theirs = theirs + lax.ppermute(far_give, "core", swap).astype(jnp.float32)

    row_masks = lax.dynamic_slice_in_dim(masks, (z_at * CORES + core) * half, half, 1)
    first = core == 0
    parts = jnp.stack([jnp.where(first, mine, theirs), jnp.where(first, theirs, mine)])
    share = parts * row_masks[:, None, :, None] * masks[:, None, None, :]
    return share.astype(jnp.bfloat16).transpose(0, 2, 1, 3)


def solution(mesh):
    op_count, sec_count = mesh.shape["op"], mesh.shape["sec"]
    split = Mesh(
        mesh.devices.reshape(op_count, sec_count // CORES, CORES), ("op", "z", "core")
    )
    placed = (
        P("op", None, None, None),
        P(),
        P(None, ("op", "z", "core"), None, None),
        P("op", None, ("z", "core"), None, None),
        P(),
    )
    return jax.shard_map(
        shards, mesh=split, in_specs=placed,
        out_specs=P("op", ("z", "core"), None, None), check_vma=False,
    )
```

```python
import functools

import jax
import jax.numpy as jnp
from jax import lax
from jax.experimental import pallas as pl
from jax.experimental.pallas import tpu as pltpu
from jax.sharding import Mesh, PartitionSpec as P

CORES = 2
GROUP = 2
ROWS = 16
LEFT_TERMS = 2
DEPTHS = (128, 192, 256)
VMEM_LIMIT = 48 << 20


def right_kernel(group, meta, site_ref, wave_ref, own_ref, other_ref, held_ref, first):
    step = pl.program_id(0)
    core, z_at, sec_count = meta[0], meta[1], meta[2]
    p_size, width = wave_ref.shape[0], wave_ref.shape[1]
    waves = wave_ref[...].reshape(p_size * width, width)
    for at in range(group):
        source = step * group + at
        for slot in range(CORES):
            side = core if slot == 0 else 1 - core
            term = source * sec_count + z_at * CORES + side
            buf = (at * CORES + slot) % 2
            first[buf] = lax.dot_general(
                waves, (own_ref if slot == 0 else other_ref)[0, at, 0],
                (((1,), (1,)), ((), ())), preferred_element_type=jnp.float32,
            )
            scale = [[site_ref[term, q * p_size + p] for p in range(p_size)] for q in range(p_size)]
            place = at * CORES + side
            for low in range(0, width, ROWS):
                parts = [first[buf, p * width + low : p * width + low + ROWS] for p in range(p_size)]
                for q in range(p_size):
                    second = parts[0] * scale[q][0]
                    for p in range(1, p_size):
                        second = second + parts[p] * scale[q][p]
                    held_ref[place, low : low + ROWS, q * width : (q + 1) * width] = second.astype(
                        jnp.bfloat16
                    )


def right_call(meta, site, wave, own, other):
    sources, width = own.shape[1], own.shape[-1]
    p_size = wave.shape[0]
    right_spec = pl.BlockSpec(
        (1, GROUP, 1, width, width), lambda step, meta: (meta[0], step, 0, 0, 0)
    )
    return pl.pallas_call(
        functools.partial(right_kernel, GROUP),
        grid_spec=pltpu.PrefetchScalarGridSpec(
            num_scalar_prefetch=1,
            grid=(sources // GROUP,),
            in_specs=[
                pl.BlockSpec(memory_space=pltpu.SMEM),
                pl.BlockSpec((p_size, width, width), lambda step, meta: (0, 0, 0)),
                right_spec,
                right_spec,
            ],
            out_specs=pl.BlockSpec(
                (GROUP * CORES, width, p_size * width), lambda step, meta: (step, 0, 0)
            ),
            scratch_shapes=[pltpu.VMEM((2, p_size * width, width), jnp.float32)],
        ),
        out_shape=jax.ShapeDtypeStruct((sources * CORES, width, p_size * width), jnp.bfloat16),
        compiler_params=pltpu.CompilerParams(vmem_limit_bytes=VMEM_LIMIT),
        name="right_terms",
    )(meta, site, wave, own, other)


def near_shifts(z_count):
    return [shift for shift in range(z_count) if shift != z_count // 2]


def left_kernel(z_count, p_size, meta, left_hbm, held_hbm, *refs):
    *outs, left, held, total, left_sem, held_sem = refs
    z_at = meta[1]
    terms, width = left.shape[0], left.shape[1]

    def accumulate(depth):
        copies = []
        for at in range(0, terms, LEFT_TERMS):
            span = pl.ds(at, LEFT_TERMS)
            slot = at // LEFT_TERMS
            used = (span, pl.ds(0, depth))
            pair = (
                pltpu.make_async_copy(left_hbm.at[span], left.at[span], left_sem.at[slot]),
                pltpu.make_async_copy(held_hbm.at[used], held.at[used], held_sem.at[slot]),
            )
            for copy in pair:
                copy.start()
            copies.append(pair)

        for slot, pair in enumerate(copies):
            for copy in pair:
                copy.wait()
            add = None
            for at in range(slot * LEFT_TERMS, (slot + 1) * LEFT_TERMS):
                product = jnp.dot(
                    left[at, :, :depth], held[at, :depth], preferred_element_type=jnp.float32
                )
                add = product if add is None else add + product
            if slot == 0:
                total[...] = add
            else:
                total[...] += add

    size, low = meta[3], 0
    for depth in DEPTHS:
        pl.when((size > low) & (size <= depth))(functools.partial(accumulate, depth))
        low = depth

    rows = width // z_count
    half = rows // CORES
    core = meta[0]

    def cut(out, shift, low, count):
        start = lax.rem(z_at + shift, z_count) * rows + low
        block = total[pl.ds(pl.multiple_of(start, half), count), :]
        for q in range(p_size):
            out[q] = block[:, q * width : (q + 1) * width].astype(out.dtype)

    far_ref, keep_ref, give_ref, *near_refs = outs
    cut(far_ref, z_count // 2, 0, rows)
    cut(keep_ref, 0, core * half, half)
    for at, shift in enumerate(near_shifts(z_count)):
        cut(give_ref.at[at], shift, (1 - core) * half, half)
        if shift:
            cut(near_refs[at - 1], shift, core * half, half)


def left_call(meta, left, held, z_count):
    terms, width, columns = held.shape
    p_size = columns // width
    rows = width // z_count
    half = (p_size, rows // CORES, width)
    near = len(near_shifts(z_count))
    out_shape = [
        jax.ShapeDtypeStruct((p_size, rows, width), jnp.bfloat16),
        jax.ShapeDtypeStruct(half, jnp.float32),
        jax.ShapeDtypeStruct((near, *half), jnp.bfloat16),
    ] + [jax.ShapeDtypeStruct(half, jnp.bfloat16)] * (near - 1)
    return pl.pallas_call(
        functools.partial(left_kernel, z_count, p_size),
        in_specs=[
            pl.BlockSpec(memory_space=pltpu.SMEM),
            pl.BlockSpec(memory_space=pl.ANY),
            pl.BlockSpec(memory_space=pl.ANY),
        ],
        out_specs=[pl.BlockSpec(memory_space=pltpu.VMEM)] * len(out_shape),
        out_shape=out_shape,
        scratch_shapes=[
            pltpu.VMEM((terms, width, width), jnp.bfloat16),
            pltpu.VMEM((terms, width, columns), jnp.bfloat16),
            pltpu.VMEM((width, columns), jnp.float32),
            pltpu.SemaphoreType.DMA((terms // LEFT_TERMS,)),
            pltpu.SemaphoreType.DMA((terms // LEFT_TERMS,)),
        ],
        compiler_params=pltpu.CompilerParams(vmem_limit_bytes=VMEM_LIMIT),
        name="left_terms",
    )(meta, left, held)


def shards(wave, sector_dims, left_ops, right_ops, site_ops):
    z_count = lax.axis_size("z")
    op_at, z_at, core = lax.axis_index("op"), lax.axis_index("z"), lax.axis_index("core")
    width, p_size = wave.shape[1], wave.shape[2]
    swap = [(0, 1), (1, 0)]

    other = lax.ppermute(right_ops, "core", swap)
    left = lax.all_to_all(left_ops[:, 0], ("op", "core"), split_axis=0, concat_axis=0, tiled=True)

    sizes = lax.dynamic_slice_in_dim(sector_dims, op_at * CORES, CORES)
    masks = (lax.broadcasted_iota(jnp.int32, (CORES, width), 1) < sizes[:, None]).astype(
        jnp.float32
    )
    mask = lax.dynamic_index_in_dim(masks, core, 0, keepdims=False)
    block = lax.dynamic_index_in_dim(wave, core, 0, keepdims=False)
    masked = block.astype(jnp.float32) * mask[:, None, None] * mask[None, None, :]
    masked = masked.astype(jnp.bfloat16).transpose(1, 0, 2)

    size = lax.dynamic_index_in_dim(sizes, core, 0, keepdims=False)
    meta = jnp.stack([core, z_at, jnp.int32(z_count * CORES), size]).astype(jnp.int32)
    site = site_ops.reshape(site_ops.shape[0], -1)
    held = right_call(meta, site, masked, right_ops, other)
    far, keep, give, *near = left_call(meta, left, held, z_count)

    def ring(block, shift):
        pairs = [(z, (z + shift) % z_count) for z in range(z_count)]
        return lax.ppermute(block, "z", pairs)

    far = ring(far, z_count // 2)
    take = lax.ppermute(give, "core", swap)
    mine, theirs = keep, take[0].astype(jnp.float32)
    for at, shift in enumerate(near_shifts(z_count)):
        if shift:
            both = ring(jnp.stack([near[at - 1], take[at]]), shift).astype(jnp.float32)
            mine, theirs = mine + both[0], theirs + both[1]
    half = keep.shape[1]
    far_mine = lax.dynamic_slice_in_dim(far, core * half, half, 1)
    far_give = lax.dynamic_slice_in_dim(far, (1 - core) * half, half, 1)
    mine = mine + far_mine.astype(jnp.float32)
    theirs = theirs + lax.ppermute(far_give, "core", swap).astype(jnp.float32)

    row_masks = lax.dynamic_slice_in_dim(masks, (z_at * CORES + core) * half, half, 1)
    first = core == 0
    parts = jnp.stack([jnp.where(first, mine, theirs), jnp.where(first, theirs, mine)])
    share = parts * row_masks[:, None, :, None] * masks[:, None, None, :]
    return share.astype(jnp.bfloat16).transpose(0, 2, 1, 3)


def solution(mesh):
    op_count, sec_count = mesh.shape["op"], mesh.shape["sec"]
    split = Mesh(
        mesh.devices.reshape(op_count, sec_count // CORES, CORES), ("op", "z", "core")
    )
    placed = (
        P("op", None, None, None),
        P(),
        P(None, ("op", "z", "core"), None, None),
        P("op", None, ("z", "core"), None, None),
        P(),
    )
    return jax.shard_map(
        shards, mesh=split, in_specs=placed,
        out_specs=P("op", ("z", "core"), None, None), check_vma=False,
    )
```

```python
import functools

import jax
import jax.numpy as jnp
from jax import lax
from jax.experimental import pallas as pl
from jax.experimental.pallas import tpu as pltpu
from jax.sharding import Mesh, PartitionSpec as P

CORES = 2
GROUP = 2
ROWS = 16
LEFT_TERMS = 2
DEPTHS = (128, 192, 256)
VMEM_LIMIT = 48 << 20


def right_kernel(group, meta, site_ref, wave_ref, own_ref, other_ref, held_ref, first):
    step = pl.program_id(0)
    core, z_at, sec_count = meta[0], meta[1], meta[2]
    p_size, width = wave_ref.shape[0], wave_ref.shape[1]
    waves = wave_ref[...].reshape(p_size * width, width)
    for at in range(group):
        source = step * group + at
        for slot in range(CORES):
            side = core if slot == 0 else 1 - core
            term = source * sec_count + z_at * CORES + side
            buf = (at * CORES + slot) % 2
            first[buf] = lax.dot_general(
                waves, (own_ref if slot == 0 else other_ref)[0, at, 0],
                (((1,), (1,)), ((), ())), preferred_element_type=jnp.float32,
            )
            scale = [[site_ref[term, q * p_size + p] for p in range(p_size)] for q in range(p_size)]
            place = at * CORES + side
            for low in range(0, width, ROWS):
                parts = [first[buf, p * width + low : p * width + low + ROWS] for p in range(p_size)]
                for q in range(p_size):
                    second = parts[0] * scale[q][0]
                    for p in range(1, p_size):
                        second = second + parts[p] * scale[q][p]
                    held_ref[place, low : low + ROWS, q * width : (q + 1) * width] = second.astype(
                        jnp.bfloat16
                    )


def right_call(meta, site, wave, own, other):
    sources, width = own.shape[1], own.shape[-1]
    p_size = wave.shape[0]
    right_spec = pl.BlockSpec(
        (1, GROUP, 1, width, width), lambda step, meta: (meta[0], step, 0, 0, 0)
    )
    return pl.pallas_call(
        functools.partial(right_kernel, GROUP),
        grid_spec=pltpu.PrefetchScalarGridSpec(
            num_scalar_prefetch=1,
            grid=(sources // GROUP,),
            in_specs=[
                pl.BlockSpec(memory_space=pltpu.SMEM),
                pl.BlockSpec((p_size, width, width), lambda step, meta: (0, 0, 0)),
                right_spec,
                right_spec,
            ],
            out_specs=pl.BlockSpec(
                (GROUP * CORES, width, p_size * width), lambda step, meta: (step, 0, 0)
            ),
            scratch_shapes=[pltpu.VMEM((2, p_size * width, width), jnp.float32)],
        ),
        out_shape=jax.ShapeDtypeStruct((sources * CORES, width, p_size * width), jnp.bfloat16),
        compiler_params=pltpu.CompilerParams(vmem_limit_bytes=VMEM_LIMIT),
        name="right_terms",
    )(meta, site, wave, own, other)


def near_shifts(z_count):
    return [shift for shift in range(z_count) if shift != z_count // 2]


def left_kernel(z_count, p_size, meta, left_hbm, held_hbm, *refs):
    *outs, left, held, total, left_sem, held_sem = refs
    z_at = meta[1]
    terms, width = left.shape[0], left.shape[1]

    def accumulate(depth):
        copies = []
        for at in range(0, terms, LEFT_TERMS):
            span = pl.ds(at, LEFT_TERMS)
            slot = at // LEFT_TERMS
            used = (span, pl.ds(0, depth))
            pair = (
                pltpu.make_async_copy(left_hbm.at[used], left.at[used], left_sem.at[slot]),
                pltpu.make_async_copy(held_hbm.at[used], held.at[used], held_sem.at[slot]),
            )
            for copy in pair:
                copy.start()
            copies.append(pair)

        for slot, pair in enumerate(copies):
            for copy in pair:
                copy.wait()
            add = None
            for at in range(slot * LEFT_TERMS, (slot + 1) * LEFT_TERMS):
                product = jnp.dot(
                    left[at, :depth, :depth], held[at, :depth], preferred_element_type=jnp.float32
                )
                add = product if add is None else add + product
            if slot == 0:
                total[:depth] = add
            else:
                total[:depth] += add
        if depth < width:
            total[depth:] = jnp.zeros_like(total[depth:])

    size, low = meta[3], 0
    for depth in DEPTHS:
        pl.when((size > low) & (size <= depth))(functools.partial(accumulate, depth))
        low = depth

    rows = width // z_count
    half = rows // CORES
    core = meta[0]

    def cut(out, shift, low, count):
        start = lax.rem(z_at + shift, z_count) * rows + low
        block = total[pl.ds(pl.multiple_of(start, half), count), :]
        for q in range(p_size):
            out[q] = block[:, q * width : (q + 1) * width].astype(out.dtype)

    far_ref, keep_ref, give_ref, *near_refs = outs
    cut(far_ref, z_count // 2, 0, rows)
    cut(keep_ref, 0, core * half, half)
    for at, shift in enumerate(near_shifts(z_count)):
        cut(give_ref.at[at], shift, (1 - core) * half, half)
        if shift:
            cut(near_refs[at - 1], shift, core * half, half)


def left_call(meta, left, held, z_count):
    terms, width, columns = held.shape
    p_size = columns // width
    rows = width // z_count
    half = (p_size, rows // CORES, width)
    near = len(near_shifts(z_count))
    out_shape = [
        jax.ShapeDtypeStruct((p_size, rows, width), jnp.bfloat16),
        jax.ShapeDtypeStruct(half, jnp.float32),
        jax.ShapeDtypeStruct((near, *half), jnp.bfloat16),
    ] + [jax.ShapeDtypeStruct(half, jnp.bfloat16)] * (near - 1)
    return pl.pallas_call(
        functools.partial(left_kernel, z_count, p_size),
        in_specs=[
            pl.BlockSpec(memory_space=pltpu.SMEM),
            pl.BlockSpec(memory_space=pl.ANY),
            pl.BlockSpec(memory_space=pl.ANY),
        ],
        out_specs=[pl.BlockSpec(memory_space=pltpu.VMEM)] * len(out_shape),
        out_shape=out_shape,
        scratch_shapes=[
            pltpu.VMEM((terms, width, width), jnp.bfloat16),
            pltpu.VMEM((terms, width, columns), jnp.bfloat16),
            pltpu.VMEM((width, columns), jnp.float32),
            pltpu.SemaphoreType.DMA((terms // LEFT_TERMS,)),
            pltpu.SemaphoreType.DMA((terms // LEFT_TERMS,)),
        ],
        compiler_params=pltpu.CompilerParams(vmem_limit_bytes=VMEM_LIMIT),
        name="left_terms",
    )(meta, left, held)


def shards(wave, sector_dims, left_ops, right_ops, site_ops):
    z_count = lax.axis_size("z")
    op_at, z_at, core = lax.axis_index("op"), lax.axis_index("z"), lax.axis_index("core")
    width, p_size = wave.shape[1], wave.shape[2]
    swap = [(0, 1), (1, 0)]

    other = lax.ppermute(right_ops, "core", swap)
    left = lax.all_to_all(left_ops[:, 0], ("op", "core"), split_axis=0, concat_axis=0, tiled=True)

    sizes = lax.dynamic_slice_in_dim(sector_dims, op_at * CORES, CORES)
    masks = (lax.broadcasted_iota(jnp.int32, (CORES, width), 1) < sizes[:, None]).astype(
        jnp.float32
    )
    mask = lax.dynamic_index_in_dim(masks, core, 0, keepdims=False)
    block = lax.dynamic_index_in_dim(wave, core, 0, keepdims=False)
    masked = block.astype(jnp.float32) * mask[:, None, None] * mask[None, None, :]
    masked = masked.astype(jnp.bfloat16).transpose(1, 0, 2)

    size = lax.dynamic_index_in_dim(sizes, core, 0, keepdims=False)
    meta = jnp.stack([core, z_at, jnp.int32(z_count * CORES), size]).astype(jnp.int32)
    site = site_ops.reshape(site_ops.shape[0], -1)
    held = right_call(meta, site, masked, right_ops, other)
    far, keep, give, *near = left_call(meta, left, held, z_count)

    def ring(block, shift):
        pairs = [(z, (z + shift) % z_count) for z in range(z_count)]
        return lax.ppermute(block, "z", pairs)

    far = ring(far, z_count // 2)
    take = lax.ppermute(give, "core", swap)
    mine, theirs = keep, take[0].astype(jnp.float32)
    for at, shift in enumerate(near_shifts(z_count)):
        if shift:
            both = ring(jnp.stack([near[at - 1], take[at]]), shift).astype(jnp.float32)
            mine, theirs = mine + both[0], theirs + both[1]
    half = keep.shape[1]
    far_mine = lax.dynamic_slice_in_dim(far, core * half, half, 1)
    far_give = lax.dynamic_slice_in_dim(far, (1 - core) * half, half, 1)
    mine = mine + far_mine.astype(jnp.float32)
    theirs = theirs + lax.ppermute(far_give, "core", swap).astype(jnp.float32)

    row_masks = lax.dynamic_slice_in_dim(masks, (z_at * CORES + core) * half, half, 1)
    first = core == 0
    parts = jnp.stack([jnp.where(first, mine, theirs), jnp.where(first, theirs, mine)])
    share = parts * row_masks[:, None, :, None] * masks[:, None, None, :]
    return share.astype(jnp.bfloat16).transpose(0, 2, 1, 3)


def solution(mesh):
    op_count, sec_count = mesh.shape["op"], mesh.shape["sec"]
    split = Mesh(
        mesh.devices.reshape(op_count, sec_count // CORES, CORES), ("op", "z", "core")
    )
    placed = (
        P("op", None, None, None),
        P(),
        P(None, ("op", "z", "core"), None, None),
        P("op", None, ("z", "core"), None, None),
        P(),
    )
    return jax.shard_map(
        shards, mesh=split, in_specs=placed,
        out_specs=P("op", ("z", "core"), None, None), check_vma=False,
    )
```

```python
import functools

import jax
import jax.numpy as jnp
from jax import lax
from jax.experimental import pallas as pl
from jax.experimental.pallas import tpu as pltpu
from jax.sharding import Mesh, PartitionSpec as P

CORES = 2
GROUP = 2
ROWS = 16
LEFT_TERMS = 2
DEPTHS = (128, 192, 256)
VMEM_LIMIT = 48 << 20


def right_kernel(group, meta, site_ref, wave_ref, own_ref, other_ref, held_ref, first):
    step = pl.program_id(0)
    core, z_at, sec_count = meta[0], meta[1], meta[2]
    p_size, width = wave_ref.shape[0], wave_ref.shape[1]
    waves = wave_ref[...].reshape(p_size * width, width)
    for at in range(group):
        source = step * group + at
        for slot in range(CORES):
            side = core if slot == 0 else 1 - core
            term = source * sec_count + z_at * CORES + side
            buf = (at * CORES + slot) % 2
            first[buf] = lax.dot_general(
                waves, (own_ref if slot == 0 else other_ref)[0, at, 0],
                (((1,), (1,)), ((), ())), preferred_element_type=jnp.float32,
            )
            scale = [[site_ref[term, q * p_size + p] for p in range(p_size)] for q in range(p_size)]
            place = at * CORES + side
            for low in range(0, width, ROWS):
                parts = [first[buf, p * width + low : p * width + low + ROWS] for p in range(p_size)]
                for q in range(p_size):
                    second = parts[0] * scale[q][0]
                    for p in range(1, p_size):
                        second = second + parts[p] * scale[q][p]
                    held_ref[place, low : low + ROWS, q * width : (q + 1) * width] = second.astype(
                        jnp.bfloat16
                    )


def right_call(meta, site, wave, own, other):
    sources, width = own.shape[1], own.shape[-1]
    p_size = wave.shape[0]
    right_spec = pl.BlockSpec(
        (1, GROUP, 1, width, width), lambda step, meta: (meta[0], step, 0, 0, 0)
    )
    return pl.pallas_call(
        functools.partial(right_kernel, GROUP),
        grid_spec=pltpu.PrefetchScalarGridSpec(
            num_scalar_prefetch=1,
            grid=(sources // GROUP,),
            in_specs=[
                pl.BlockSpec(memory_space=pltpu.SMEM),
                pl.BlockSpec((p_size, width, width), lambda step, meta: (0, 0, 0)),
                right_spec,
                right_spec,
            ],
            out_specs=pl.BlockSpec(
                (GROUP * CORES, width, p_size * width), lambda step, meta: (step, 0, 0)
            ),
            scratch_shapes=[pltpu.VMEM((2, p_size * width, width), jnp.float32)],
        ),
        out_shape=jax.ShapeDtypeStruct((sources * CORES, width, p_size * width), jnp.bfloat16),
        compiler_params=pltpu.CompilerParams(vmem_limit_bytes=VMEM_LIMIT),
        name="right_terms",
    )(meta, site, wave, own, other)


def near_shifts(z_count):
    return [shift for shift in range(1, z_count) if shift != z_count // 2]


def left_kernel(z_count, p_size, meta, left_hbm, held_hbm, *refs):
    *outs, left, held, total, left_sem, held_sem = refs
    z_at = meta[1]
    terms, width = left.shape[0], left.shape[1]

    def accumulate(depth):
        copies = []
        for at in range(0, terms, LEFT_TERMS):
            span = pl.ds(at, LEFT_TERMS)
            slot = at // LEFT_TERMS
            used = (span, pl.ds(0, depth))
            pair = (
                pltpu.make_async_copy(left_hbm.at[used], left.at[used], left_sem.at[slot]),
                pltpu.make_async_copy(held_hbm.at[used], held.at[used], held_sem.at[slot]),
            )
            for copy in pair:
                copy.start()
            copies.append(pair)

        for slot, pair in enumerate(copies):
            for copy in pair:
                copy.wait()
            add = None
            for at in range(slot * LEFT_TERMS, (slot + 1) * LEFT_TERMS):
                product = jnp.dot(
                    left[at, :depth, :depth], held[at, :depth], preferred_element_type=jnp.float32
                )
                add = product if add is None else add + product
            if slot == 0:
                total[:depth] = add
            else:
                total[:depth] += add
        if depth < width:
            total[depth:] = jnp.zeros_like(total[depth:])

    size, low = meta[3], 0
    for depth in DEPTHS:
        pl.when((size > low) & (size <= depth))(functools.partial(accumulate, depth))
        low = depth

    rows = width // z_count
    half = rows // CORES
    core = meta[0]

    def cut(out, shift, low, count):
        start = lax.rem(z_at + shift, z_count) * rows + low
        block = total[pl.ds(pl.multiple_of(start, half), count), :]
        for q in range(p_size):
            out[q] = block[:, q * width : (q + 1) * width].astype(out.dtype)

    keep_ref, far_ref, give_ref, *near_refs = outs
    for at, (shift, out) in enumerate(((0, keep_ref), (z_count // 2, far_ref))):
        cut(out, shift, core * half, half)
        cut(give_ref.at[at], shift, (1 - core) * half, half)
    for shift, out in zip(near_shifts(z_count), near_refs):
        cut(out, shift, 0, rows)


def left_call(meta, left, held, z_count):
    terms, width, columns = held.shape
    p_size = columns // width
    rows = width // z_count
    half = (p_size, rows // CORES, width)
    block = jax.ShapeDtypeStruct((p_size, rows, width), jnp.bfloat16)
    out_shape = [
        jax.ShapeDtypeStruct(half, jnp.float32),
        jax.ShapeDtypeStruct(half, jnp.bfloat16),
        jax.ShapeDtypeStruct((2, *half), jnp.bfloat16),
    ] + [block] * len(near_shifts(z_count))
    return pl.pallas_call(
        functools.partial(left_kernel, z_count, p_size),
        in_specs=[
            pl.BlockSpec(memory_space=pltpu.SMEM),
            pl.BlockSpec(memory_space=pl.ANY),
            pl.BlockSpec(memory_space=pl.ANY),
        ],
        out_specs=[pl.BlockSpec(memory_space=pltpu.VMEM)] * len(out_shape),
        out_shape=out_shape,
        scratch_shapes=[
            pltpu.VMEM((terms, width, width), jnp.bfloat16),
            pltpu.VMEM((terms, width, columns), jnp.bfloat16),
            pltpu.VMEM((width, columns), jnp.float32),
            pltpu.SemaphoreType.DMA((terms // LEFT_TERMS,)),
            pltpu.SemaphoreType.DMA((terms // LEFT_TERMS,)),
        ],
        compiler_params=pltpu.CompilerParams(vmem_limit_bytes=VMEM_LIMIT),
        name="left_terms",
    )(meta, left, held)


def shards(wave, sector_dims, left_ops, right_ops, site_ops):
    z_count = lax.axis_size("z")
    op_at, z_at, core = lax.axis_index("op"), lax.axis_index("z"), lax.axis_index("core")
    width, p_size = wave.shape[1], wave.shape[2]
    swap = [(0, 1), (1, 0)]

    other = lax.ppermute(right_ops, "core", swap)
    left = lax.all_to_all(left_ops[:, 0], ("op", "core"), split_axis=0, concat_axis=0, tiled=True)

    sizes = lax.dynamic_slice_in_dim(sector_dims, op_at * CORES, CORES)
    masks = (lax.broadcasted_iota(jnp.int32, (CORES, width), 1) < sizes[:, None]).astype(
        jnp.float32
    )
    mask = lax.dynamic_index_in_dim(masks, core, 0, keepdims=False)
    block = lax.dynamic_index_in_dim(wave, core, 0, keepdims=False)
    masked = block.astype(jnp.float32) * mask[:, None, None] * mask[None, None, :]
    masked = masked.astype(jnp.bfloat16).transpose(1, 0, 2)

    size = lax.dynamic_index_in_dim(sizes, core, 0, keepdims=False)
    meta = jnp.stack([core, z_at, jnp.int32(z_count * CORES), size]).astype(jnp.int32)
    site = site_ops.reshape(site_ops.shape[0], -1)
    held = right_call(meta, site, masked, right_ops, other)
    keep, far, give, *near = left_call(meta, left, held, z_count)
    half = keep.shape[1]

    def ring(block, shift):
        pairs = [(z, (z + shift) % z_count) for z in range(z_count)]
        return lax.ppermute(block, "z", pairs)

    near = [ring(block, shift) for shift, block in zip(near_shifts(z_count), near)]
    take = lax.ppermute(give, "core", swap)
    both = ring(jnp.stack([far, take[1]]), z_count // 2).astype(jnp.float32)
    mine = keep + both[0]
    theirs = take[0].astype(jnp.float32) + both[1]
    for block in near:
        stay = lax.dynamic_slice_in_dim(block, core * half, half, 1)
        leave = lax.dynamic_slice_in_dim(block, (1 - core) * half, half, 1)
        mine = mine + stay.astype(jnp.float32)
        theirs = theirs + lax.ppermute(leave, "core", swap).astype(jnp.float32)

    row_masks = lax.dynamic_slice_in_dim(masks, (z_at * CORES + core) * half, half, 1)
    first = core == 0
    parts = jnp.stack([jnp.where(first, mine, theirs), jnp.where(first, theirs, mine)])
    share = parts * row_masks[:, None, :, None] * masks[:, None, None, :]
    return share.astype(jnp.bfloat16).transpose(0, 2, 1, 3)


def solution(mesh):
    op_count, sec_count = mesh.shape["op"], mesh.shape["sec"]
    split = Mesh(
        mesh.devices.reshape(op_count, sec_count // CORES, CORES), ("op", "z", "core")
    )
    placed = (
        P("op", None, None, None),
        P(),
        P(None, ("op", "z", "core"), None, None),
        P("op", None, ("z", "core"), None, None),
        P(),
    )
    return jax.shard_map(
        shards, mesh=split, in_specs=placed,
        out_specs=P("op", ("z", "core"), None, None), check_vma=False,
    )
```

```python
import functools

import jax
import jax.numpy as jnp
from jax import lax
from jax.experimental import pallas as pl
from jax.experimental.pallas import tpu as pltpu
from jax.sharding import Mesh, PartitionSpec as P

CORES = 2
GROUP = 2
ROWS = 16
LEFT_TERMS = 2
DEPTHS = (128, 192, 256)
VMEM_LIMIT = 48 << 20


def right_kernel(group, meta, site_ref, wave_ref, own_ref, other_ref, held_ref, first):
    step = pl.program_id(0)
    core, z_at, sec_count = meta[0], meta[1], meta[2]
    p_size, width = wave_ref.shape[0], wave_ref.shape[1]
    waves = wave_ref[...].reshape(p_size * width, width)
    for at in range(group):
        source = step * group + at
        for slot in range(CORES):
            side = core if slot == 0 else 1 - core
            term = source * sec_count + z_at * CORES + side
            buf = (at * CORES + slot) % 2
            first[buf] = lax.dot_general(
                waves, (own_ref if slot == 0 else other_ref)[0, at, 0],
                (((1,), (1,)), ((), ())), preferred_element_type=jnp.float32,
            )
            scale = [[site_ref[term, q * p_size + p] for p in range(p_size)] for q in range(p_size)]
            place = at * CORES + side
            for low in range(0, width, ROWS):
                parts = [first[buf, p * width + low : p * width + low + ROWS] for p in range(p_size)]
                for q in range(p_size):
                    second = parts[0] * scale[q][0]
                    for p in range(1, p_size):
                        second = second + parts[p] * scale[q][p]
                    held_ref[place, low : low + ROWS, q * width : (q + 1) * width] = second.astype(
                        jnp.bfloat16
                    )


def right_call(meta, site, wave, own, other):
    sources, width = own.shape[1], own.shape[-1]
    p_size = wave.shape[0]
    right_spec = pl.BlockSpec(
        (1, GROUP, 1, width, width), lambda step, meta: (meta[0], step, 0, 0, 0)
    )
    return pl.pallas_call(
        functools.partial(right_kernel, GROUP),
        grid_spec=pltpu.PrefetchScalarGridSpec(
            num_scalar_prefetch=1,
            grid=(sources // GROUP,),
            in_specs=[
                pl.BlockSpec(memory_space=pltpu.SMEM),
                pl.BlockSpec((p_size, width, width), lambda step, meta: (0, 0, 0)),
                right_spec,
                right_spec,
            ],
            out_specs=pl.BlockSpec(
                (GROUP * CORES, width, p_size * width), lambda step, meta: (step, 0, 0)
            ),
            scratch_shapes=[pltpu.VMEM((2, p_size * width, width), jnp.float32)],
        ),
        out_shape=jax.ShapeDtypeStruct((sources * CORES, width, p_size * width), jnp.bfloat16),
        compiler_params=pltpu.CompilerParams(vmem_limit_bytes=VMEM_LIMIT),
        name="right_terms",
    )(meta, site, wave, own, other)


def near_shifts(z_count):
    return [shift for shift in range(z_count) if shift != z_count // 2]


def left_kernel(z_count, p_size, meta, left_hbm, held_hbm, *refs):
    *outs, left, held, total, left_sem, held_sem = refs
    z_at = meta[1]
    terms, width = left.shape[0], left.shape[1]

    def accumulate(depth):
        copies = []
        lows = [0] + list(range(1, terms, LEFT_TERMS))
        ends = lows[1:] + [terms]
        for slot, (at, end) in enumerate(zip(lows, ends)):
            span = pl.ds(at, end - at)
            used = (span, pl.ds(0, depth))
            pair = (
                pltpu.make_async_copy(left_hbm.at[used], left.at[used], left_sem.at[slot]),
                pltpu.make_async_copy(held_hbm.at[used], held.at[used], held_sem.at[slot]),
            )
            for copy in pair:
                copy.start()
            copies.append(pair)

        for slot, pair in enumerate(copies):
            for copy in pair:
                copy.wait()
            add = None
            for at in range(lows[slot], ends[slot]):
                product = jnp.dot(
                    left[at, :depth, :depth], held[at, :depth], preferred_element_type=jnp.float32
                )
                add = product if add is None else add + product
            if slot == 0:
                total[:depth] = add
            else:
                total[:depth] += add
        if depth < width:
            total[depth:] = jnp.zeros_like(total[depth:])

    size, low = meta[3], 0
    for depth in DEPTHS:
        pl.when((size > low) & (size <= depth))(functools.partial(accumulate, depth))
        low = depth

    rows = width // z_count
    half = rows // CORES
    core = meta[0]

    def cut(out, shift, low, count):
        start = lax.rem(z_at + shift, z_count) * rows + low
        block = total[pl.ds(pl.multiple_of(start, half), count), :]
        for q in range(p_size):
            out[q] = block[:, q * width : (q + 1) * width].astype(out.dtype)

    far_ref, keep_ref, give_ref, *near_refs = outs
    cut(far_ref, z_count // 2, 0, rows)
    cut(keep_ref, 0, core * half, half)
    for at, shift in enumerate(near_shifts(z_count)):
        cut(give_ref.at[at], shift, (1 - core) * half, half)
        if shift:
            cut(near_refs[at - 1], shift, core * half, half)


def left_call(meta, left, held, z_count):
    terms, width, columns = held.shape
    p_size = columns // width
    rows = width // z_count
    half = (p_size, rows // CORES, width)
    near = len(near_shifts(z_count))
    out_shape = [
        jax.ShapeDtypeStruct((p_size, rows, width), jnp.bfloat16),
        jax.ShapeDtypeStruct(half, jnp.float32),
        jax.ShapeDtypeStruct((near, *half), jnp.bfloat16),
    ] + [jax.ShapeDtypeStruct(half, jnp.bfloat16)] * (near - 1)
    return pl.pallas_call(
        functools.partial(left_kernel, z_count, p_size),
        in_specs=[
            pl.BlockSpec(memory_space=pltpu.SMEM),
            pl.BlockSpec(memory_space=pl.ANY),
            pl.BlockSpec(memory_space=pl.ANY),
        ],
        out_specs=[pl.BlockSpec(memory_space=pltpu.VMEM)] * len(out_shape),
        out_shape=out_shape,
        scratch_shapes=[
            pltpu.VMEM((terms, width, width), jnp.bfloat16),
            pltpu.VMEM((terms, width, columns), jnp.bfloat16),
            pltpu.VMEM((width, columns), jnp.float32),
            pltpu.SemaphoreType.DMA((terms // LEFT_TERMS + 1,)),
            pltpu.SemaphoreType.DMA((terms // LEFT_TERMS + 1,)),
        ],
        compiler_params=pltpu.CompilerParams(vmem_limit_bytes=VMEM_LIMIT),
        name="left_terms",
    )(meta, left, held)


def shards(wave, sector_dims, left_ops, right_ops, site_ops):
    z_count = lax.axis_size("z")
    op_at, z_at, core = lax.axis_index("op"), lax.axis_index("z"), lax.axis_index("core")
    width, p_size = wave.shape[1], wave.shape[2]
    swap = [(0, 1), (1, 0)]

    other = lax.ppermute(right_ops, "core", swap)
    left = lax.all_to_all(left_ops[:, 0], ("op", "core"), split_axis=0, concat_axis=0, tiled=True)

    sizes = lax.dynamic_slice_in_dim(sector_dims, op_at * CORES, CORES)
    masks = (lax.broadcasted_iota(jnp.int32, (CORES, width), 1) < sizes[:, None]).astype(
        jnp.float32
    )
    mask = lax.dynamic_index_in_dim(masks, core, 0, keepdims=False)
    block = lax.dynamic_index_in_dim(wave, core, 0, keepdims=False)
    masked = block.astype(jnp.float32) * mask[:, None, None] * mask[None, None, :]
    masked = masked.astype(jnp.bfloat16).transpose(1, 0, 2)

    size = lax.dynamic_index_in_dim(sizes, core, 0, keepdims=False)
    meta = jnp.stack([core, z_at, jnp.int32(z_count * CORES), size]).astype(jnp.int32)
    site = site_ops.reshape(site_ops.shape[0], -1)
    held = right_call(meta, site, masked, right_ops, other)
    far, keep, give, *near = left_call(meta, left, held, z_count)

    def ring(block, shift):
        pairs = [(z, (z + shift) % z_count) for z in range(z_count)]
        return lax.ppermute(block, "z", pairs)

    far = ring(far, z_count // 2)
    take = lax.ppermute(give, "core", swap)
    mine, theirs = keep, take[0].astype(jnp.float32)
    for at, shift in enumerate(near_shifts(z_count)):
        if shift:
            both = ring(jnp.stack([near[at - 1], take[at]]), shift).astype(jnp.float32)
            mine, theirs = mine + both[0], theirs + both[1]
    half = keep.shape[1]
    far_mine = lax.dynamic_slice_in_dim(far, core * half, half, 1)
    far_give = lax.dynamic_slice_in_dim(far, (1 - core) * half, half, 1)
    mine = mine + far_mine.astype(jnp.float32)
    theirs = theirs + lax.ppermute(far_give, "core", swap).astype(jnp.float32)

    row_masks = lax.dynamic_slice_in_dim(masks, (z_at * CORES + core) * half, half, 1)
    first = core == 0
    parts = jnp.stack([jnp.where(first, mine, theirs), jnp.where(first, theirs, mine)])
    share = parts * row_masks[:, None, :, None] * masks[:, None, None, :]
    return share.astype(jnp.bfloat16).transpose(0, 2, 1, 3)


def solution(mesh):
    op_count, sec_count = mesh.shape["op"], mesh.shape["sec"]
    split = Mesh(
        mesh.devices.reshape(op_count, sec_count // CORES, CORES), ("op", "z", "core")
    )
    placed = (
        P("op", None, None, None),
        P(),
        P(None, ("op", "z", "core"), None, None),
        P("op", None, ("z", "core"), None, None),
        P(),
    )
    return jax.shard_map(
        shards, mesh=split, in_specs=placed,
        out_specs=P("op", ("z", "core"), None, None), check_vma=False,
    )
```
